32 devices in a mesh: grp: 4 (over x, core), col: 8 (over z, y).
Axes of the slice: x: 2, y: 2, z: 4, core: 2. Of those that a mesh axis runs over, the one named last changes fastest.
Arguments:
- diag_blocks: float32 [4096, 1024], P('grp', 'col'), may hold values from -8 to 48, as said below
- coupling: float32 [24576, 1024], P(('grp', 'col')), may hold values from -4 to 4
- parent_front: float32 [12288, 12288], P('grp', 'col'), may hold values from -6 to 6
- index_maps: int32 [4, 48], replicated, may hold values from 0 to 95, as said below
Outputs:
- assembled: float32 [12288, 12288], P('grp', 'col')
- diag_factor: float32 [4096, 1024], P('grp', 'col')
- panel: float32 [24576, 1024], P(('grp', 'col'))
The draws below stay inside these ranges and needn't reach their ends.
Inputs may be any that keep to these rules, and one draw needn't show every extreme that they name: `diag_blocks`: each front's block of 1024 rows is symmetric positive definite. `index_maps`: the 48 entries of one row are distinct, and every parent block is named by some front.
All inputs are finite; a program needn't handle non-finite values.
Results may differ from the reference program's by a relative error of at most 0.0027.
Values may be sent and summed in bfloat16 or wider, within the bound.
No kernel may reach another device: no remote copies, remote signals or barrier semaphores. Data moves between devices by JAX's collectives and lax.ppermute only.
A program may use at most 192 MiB of HBM per device.

```python
import math
import jax
import jax.numpy as jnp
from jax import lax

FRONTS = 4
PIV = 1024
SCH = 6144
BLK = 128
NPAR = 12288
SBLK = 48
PBLK = 96


def draw_diag_blocks(key, part):
    subkeys = jax.random.split(key, 2)
    noise_draw = jax.random.truncated_normal(subkeys[0], -3.0, 3.0, (FRONTS, PIV, PIV), jnp.float32)
    symmetric = (noise_draw + jnp.swapaxes(noise_draw, 1, 2)) * (0.5 / math.sqrt(2.0 * PIV))
    diag_vals = jax.random.uniform(subkeys[1], (FRONTS, PIV), jnp.float32, 1.8, 2.6)
    matrix = symmetric + diag_vals[:, :, None] * jnp.eye(PIV, dtype=jnp.float32)[None, :, :]
    return matrix.reshape(FRONTS * PIV, PIV)


def draw_index_maps(key, part):
    subkeys = jax.random.split(key, 3)
    parent_order = jax.random.permutation(subkeys[0], PBLK)
    crowded = 3 * PBLK // 4
    front_zero = parent_order[:SBLK]
    front_one = parent_order[SBLK:2 * SBLK]
    front_two = parent_order[jax.random.permutation(subkeys[1], crowded)[:SBLK]]
    front_three = parent_order[jax.random.permutation(subkeys[2], crowded)[:SBLK]]
    return jnp.stack([front_zero, front_one, front_two, front_three], axis=0).astype(jnp.int32)


def level_of(stream_key, shape, cuts, low, top_value):
    loudness = 1.0
    for position, blocks in cuts:
        steps = jax.random.uniform(jax.random.fold_in(jax.random.fold_in(stream_key, 6), position), (blocks,), jnp.float32, low / len(cuts), top_value / len(cuts))
        loudness = loudness * jnp.repeat(jnp.exp(steps), shape[position] // blocks).reshape((-1,) + (1,) * (len(shape) - 1 - position))
    return loudness


def scatter_about(stream_key, extent, deviation, most, pieces=(), kind=jnp.bfloat16):
    values = deviation * jax.random.normal(stream_key, extent, jnp.float32)
    if pieces:
        values = values * level_of(stream_key, extent, pieces, -0.22, 0.18)
    return jnp.clip(values, -most, most).astype(kind)


def setup_inputs(seed: int = 0) -> dict:
    seeds = jax.random.split(jax.random.key(seed), 5)
    diag_blocks = draw_diag_blocks(jax.random.fold_in(seeds[4], 71), 0)
    coupling = scatter_about(seeds[1], (FRONTS * SCH, PIV), (1.5 * PIV ** -0.25), 4.0, ((0, 32),), jnp.float32)
    parent_front = scatter_about(seeds[2], (NPAR, NPAR), 1.0, 6.0, ((0, 4), (1, 8)), jnp.float32)
    index_maps = draw_index_maps(jax.random.fold_in(seeds[4], 71), 0)
    return {"diag_blocks": diag_blocks, "coupling": coupling, "parent_front": parent_front, "index_maps": index_maps}


def reference(diag_blocks, coupling, parent_front, index_maps):
    factor_list = []
    panel_list = []
    assembled = parent_front.reshape(PBLK, BLK, PBLK, BLK)
    for front_id in range(FRONTS):
        block_a = diag_blocks[front_id * PIV:(front_id + 1) * PIV]
        lower_factor = jnp.linalg.cholesky(block_a)
        coupling_rows = coupling[front_id * SCH:(front_id + 1) * SCH]
        panel_rows = lax.linalg.triangular_solve(lower_factor, coupling_rows, left_side=False, lower=True, transpose_a=True)
        rounded = panel_rows.astype(jnp.bfloat16)
        update = jnp.dot(rounded.astype(jnp.float32), rounded.T.astype(jnp.float32), preferred_element_type=jnp.float32)
        update = update.reshape(SBLK, BLK, SBLK, BLK).transpose(0, 2, 1, 3)
        targets = index_maps[front_id].astype(jnp.int32)
        assembled = assembled.at[targets[:, None], :, targets[None, :], :].add(-update)
        factor_list.append(lower_factor)
        panel_list.append(panel_rows)
    return (assembled.reshape(NPAR, NPAR), jnp.concatenate(factor_list, axis=0), jnp.concatenate(panel_list, axis=0))
```

```python
import functools

import jax
import jax.numpy as jnp
from jax import lax
from jax.experimental import pallas as pl
from jax.experimental.pallas import tpu as pltpu
from jax.sharding import PartitionSpec as P

FRONTS = 4
BLK = 128
SBLK = 48
PBLK = 96
F32 = jnp.float32
HALF = jnp.bfloat16
EXACT = lax.Precision.HIGHEST
ANY = pl.BlockSpec(memory_space=pl.ANY)


def swapped(block, axis, stride):
    count = lax.axis_size(axis)
    route = []
    for low in range(count):
        high = low | 1 << stride
        if high != low and high < count:
            route += [(low, high), (high, low)]
    return lax.ppermute(block, axis, route)


def place_rows(slab_blocks, source_block, present_count, count):
    picked = slab_blocks[jnp.arange(FRONTS)[:, None], source_block]
    picked = jnp.where(present_count[:, :, None, None] > 0, picked, jnp.zeros_like(picked))
    return jnp.transpose(picked, (1, 2, 0, 3)).reshape(count * BLK, -1)


def general(diag_blocks, coupling, parent_front, index_maps):
    groups = lax.axis_size("grp") // FRONTS
    swap_depth = groups.bit_length() - 1
    grp_index = lax.axis_index("grp")
    col_index = lax.axis_index("col")
    gathered = lax.all_gather(diag_blocks, "col", axis=1, tiled=True)
    for bit_pos in range(swap_depth):
        partner = swapped(gathered, "grp", bit_pos)
        is_upper = grp_index // 2**bit_pos % 2 == 1
        lower_half = jnp.where(is_upper, partner, gathered)
        upper_half = jnp.where(is_upper, gathered, partner)
        gathered = jnp.concatenate([lower_half, upper_half], axis=0)
    factor = jnp.linalg.cholesky(gathered)
    rows_here = diag_blocks.shape[0]
    col_width = diag_blocks.shape[1]
    local_start = grp_index % groups * rows_here
    factor_tile = lax.dynamic_slice(
        factor, (local_start, col_index * col_width), (rows_here, col_width)
    )
    panel_rows = lax.linalg.triangular_solve(
        factor, coupling, left_side=False, lower=True, transpose_a=True
    )
    panel_half = panel_rows.astype(HALF)
    panel_tiles = lax.all_to_all(panel_half, "col", split_axis=1, concat_axis=0, tiled=True)
    panel_slab = lax.all_gather(panel_tiles, "grp", axis=0, tiled=True)
    slab_blocks = panel_slab.reshape(FRONTS, SBLK, BLK, -1)
    parent_ids = jnp.arange(PBLK, dtype=jnp.int32)
    matches = (index_maps[:, :, None] == parent_ids[None, None, :]).astype(jnp.int32)
    present_count = jnp.sum(matches, axis=1)
    source_block = jnp.sum(matches * jnp.arange(SBLK, dtype=jnp.int32)[None, :, None], axis=1)
    row_count = parent_front.shape[0]
    contract = (((1,), (1,)), ((), ()))
    every_part = place_rows(slab_blocks, source_block, present_count, PBLK)
    col_operand = lax.all_to_all(every_part, "col", split_axis=0, concat_axis=1, tiled=True)
    row_part = lax.dynamic_slice_in_dim(every_part, grp_index * row_count, row_count, 0)
    update = lax.dot_general(
        lax.all_gather(row_part, "col", axis=1, tiled=True),
        col_operand,
        contract,
        preferred_element_type=F32,
    )
    return (parent_front - update, factor_tile, panel_rows)


def dot(a, b, ca, cb):
    return lax.dot_general(
        a, b, (((ca,), (cb,)), ((), ())), precision=EXACT, preferred_element_type=F32
    )


def eliminate(s_val, u_ref, inv_ref, width):
    rows = 8
    shape = (width, width)
    eye = lax.broadcasted_iota(jnp.int32, shape, 0) == lax.broadcasted_iota(jnp.int32, shape, 1)
    sub = lax.broadcasted_iota(jnp.int32, (rows, 1), 0)

    def group(g, carry):
        s, e = carry
        scale = jnp.zeros((rows, 1), F32)
        for i in range(rows):
            pivot = s[i : i + 1, i : i + 1]
            s_row, e_row = s[i : i + 1, :], e[i : i + 1, :]
            mult = s[:, i : i + 1] * (1.0 / pivot)
            below = jnp.where(sub > i, mult[:rows], 0.0)
            mult = jnp.concatenate([below, mult[rows:]], axis=0)
            s = s - mult * s_row
            e = e - mult * e_row
            scale = jnp.where(sub == i, lax.rsqrt(pivot), scale)
        at = pl.multiple_of(g * rows, rows)
        u_ref[pl.ds(at, rows), :] = pltpu.roll(s[:rows] * scale, at, 1)
        inv_ref[pl.ds(at, rows), :] = e[:rows] * scale
        s = jnp.concatenate([s[rows:], s[:rows]], axis=0)
        e = jnp.concatenate([e[rows:], e[:rows]], axis=0)
        return pltpu.roll(s, width - rows, 1), e

    lax.fori_loop(0, width // rows, group, (s_val, eye.astype(F32)))


def factor_body(k, width, cols, col_ref, *refs):
    pieces, c_ref, refs = refs[:cols], refs[cols], refs[cols + 1 :]
    if k:
        u_in, x_in, refs = refs[0], refs[1], refs[2:]
    u_out, x_out, half_ref, u_v, x_v, s_v, t_v, uk_v, inv_v, sem = refs
    n = s_v.shape[1]
    base = k * width
    rest = n - base - width
    here = pl.ds(base, width)
    if k:
        before = pl.ds(0, base)
        load_u = pltpu.make_async_copy(u_in.at[before, :], u_v.at[before, :], sem.at[0])
        load_x = pltpu.make_async_copy(x_in.at[:, before], x_v.at[:, before], sem.at[1])
        load_u.start()
        load_x.start()
    for rel in range(cols):
        at = pl.multiple_of((col_ref[0] ^ rel) * width, width)
        s_v[:, pl.ds(at, width)] = pieces[rel][...]
    if k:
        load_u.wait()

        def prev(j, _):
            at = pl.multiple_of(j * width, width)
            uj = u_v[pl.ds(at, width), pl.ds(base, n - base)]
            s_v[:, pl.ds(base, n - base)] -= dot(uj[:, :width], uj, 0, 0)
            return 0

        lax.fori_loop(0, k, prev, 0)
    eliminate(s_v[:, here], uk_v, inv_v, width)
    inv = inv_v[...]
    r = lax.broadcasted_iota(jnp.int32, (width, width), 0)
    c = lax.broadcasted_iota(jnp.int32, (width, width), 1)
    if base:
        u_v[here, pl.ds(0, base)] = jnp.zeros((width, base), F32)
    u_v[here, here] = jnp.where(c >= r, uk_v[...], 0.0)
    if rest:
        right = pl.ds(base + width, rest)
        u_v[here, right] = dot(inv, s_v[:, right], 1, 0)
    save_u = pltpu.make_async_copy(u_v.at[here, :], u_out.at[here, :], sem.at[2])
    save_u.start()
    t_v[...] = c_ref[...]
    if k:
        load_x.wait()

        def prevx(j, _):
            at = pl.multiple_of(j * width, width)
            t_v[...] -= dot(x_v[:, pl.ds(at, width)], u_v[pl.ds(at, width), here], 1, 0)
            return 0

        lax.fori_loop(0, k, prevx, 0)
    x_v[:, here] = dot(t_v[...], inv, 1, 1)
    half_ref[...] = x_v[:, here].astype(HALF)
    save_x = pltpu.make_async_copy(x_v.at[:, here], x_out.at[:, here], sem.at[3])
    save_x.start()
    save_u.wait()
    save_x.wait()


def factor_step(k, first, pieces, coupling, u_all, x_all, col_id):
    m, n = coupling.shape
    width = pieces[0].shape[1]
    cols = len(pieces)
    args = [*pieces, coupling]
    specs = [pl.BlockSpec((width, width), lambda i, s: (k - first, 0))] * cols
    specs += [pl.BlockSpec((m, width), lambda i, s: (0, k))]
    alias = {}
    if k:
        alias = {len(args) + 1: 0, len(args) + 2: 1}
        args += [u_all, x_all]
        specs += [ANY, ANY]
    square = pltpu.VMEM((width, width), F32)
    return pl.pallas_call(
        functools.partial(factor_body, k, width, cols),
        grid_spec=pltpu.PrefetchScalarGridSpec(
            num_scalar_prefetch=1,
            grid=(1,),
            in_specs=specs,
            out_specs=(ANY, ANY, pl.BlockSpec((m, width), lambda i, s: (0, 0))),
            scratch_shapes=[
                pltpu.VMEM((n, n), F32),
                pltpu.VMEM((m, n), F32),
                pltpu.VMEM((width, n), F32),
                pltpu.VMEM((m, width), F32),
                square,
                square,
                pltpu.SemaphoreType.DMA((4,)),
            ],
        ),
        out_shape=(
            jax.ShapeDtypeStruct((n, n), F32),
            jax.ShapeDtypeStruct((m, n), F32),
            jax.ShapeDtypeStruct((m, width), HALF),
        ),
        input_output_aliases=alias,
        compiler_params=pltpu.CompilerParams(vmem_limit_bytes=32 << 20),
        cost_estimate=pl.CostEstimate(
            flops=10**9, bytes_accessed=48 << 20, transcendentals=0
        ),
        name=f"factor{k}",
    )(col_id, *args)


def extend_body(count, per, split, maps, place, parent, *refs):
    arrays, refs = refs[: count * split], refs[count * split :]
    out, acc, lhs, rhs, lists, sem, acc_sem = refs
    rows, cols = parent.shape
    nrb, ncb = rows // BLK, cols // BLK
    width = arrays[0].shape[1]
    load = pltpu.make_async_copy(parent, acc, acc_sem.at[0])
    load.start()
    grp, col, zs = place[0], place[1], place[2]
    x_at, core_at = grp // 2, grp % 2

    def locate(f, i):
        src = i // per
        dc = (f % 2) ^ core_at
        dx = (f // 2) ^ x_at
        dcol = src ^ col
        dy = dcol % 2
        dz = dcol // 2
        near = jnp.where((core_at ^ dc) == 0, dx + 2 * dy, dy + 2 * dx)
        return 4 * dc + near, (dz * per + i % per) * BLK

    def fetch(f, slot):
        def scan(i, state):
            nr, nc = state
            p = maps[f, i]
            which, start = locate(f, i)
            start = pl.multiple_of(start, BLK)
            in_rows = p // nrb == grp
            in_cols = p // ncb == col

            @pl.when(in_rows)
            def _():
                lists[slot, nr] = p % nrb

            @pl.when(in_cols)
            def _():
                lists[slot, nrb + nc] = p % ncb

            @pl.when(in_rows | in_cols)
            def _():
                for a in range(split):

                    @pl.when(which == a)
                    def _():
                        for n in range(count):
                            src = arrays[n * split + a].at[pl.ds(start, BLK), :]
                            where = pl.ds(n * width, width)

                            @pl.when(in_rows)
                            def _():
                                at = pl.ds(pl.multiple_of(nr * BLK, BLK), BLK)
                                pltpu.make_async_copy(
                                    src, lhs.at[slot, at, where], sem.at[slot]
                                ).start()

                            @pl.when(in_cols)
                            def _():
                                at = pl.ds(pl.multiple_of(nc * BLK, BLK), BLK)
                                pltpu.make_async_copy(
                                    src, rhs.at[slot, at, where], sem.at[slot]
                                ).start()

            return nr + in_rows.astype(jnp.int32), nc + in_cols.astype(jnp.int32)

        zero = jnp.int32(0)
        nr, nc = lax.fori_loop(0, maps.shape[1], scan, (zero, zero))
        lists[slot, nrb + ncb] = nr
        lists[slot, nrb + ncb + 1] = nc

    def drain(slot):
        total = lists[slot, nrb + ncb] + lists[slot, nrb + ncb + 1]

        def one(_, carry):
            block = lhs.at[slot, pl.ds(0, BLK), :]
            pltpu.make_async_copy(block, block, sem.at[slot]).wait()
            return carry

        lax.fori_loop(0, total, one, 0)

    fetch(0, 0)
    for f in range(FRONTS):
        slot = f % 2
        if f + 1 < FRONTS:
            fetch(f + 1, 1 - slot)
        drain(slot)
        if f == 0:
            load.wait()
        nr, nc = lists[slot, nrb + ncb], lists[slot, nrb + ncb + 1]
        tall, wide = 4, 2

        def col_step(j, _):
            right = rhs[slot, pl.ds(pl.multiple_of(j * wide * BLK, wide * BLK), wide * BLK), :]

            def row_step(i, _):
                left = lhs[slot, pl.ds(pl.multiple_of(i * tall * BLK, tall * BLK), tall * BLK), :]
                prod = lax.dot_general(
                    left, right, (((1,), (1,)), ((), ())), preferred_element_type=F32
                )
                for b in range(wide):
                    for a in range(tall):

                        @pl.when((i * tall + a < nr) & (j * wide + b < nc))
                        def _():
                            r = pl.multiple_of(lists[slot, i * tall + a] * BLK, BLK)
                            c = pl.multiple_of(lists[slot, nrb + j * wide + b] * BLK, BLK)
                            acc[pl.ds(r, BLK), pl.ds(c, BLK)] -= prod[
                                a * BLK : (a + 1) * BLK, b * BLK : (b + 1) * BLK
                            ]

                return 0

            lax.fori_loop(0, (nr + tall - 1) // tall, row_step, 0)
            return 0

        lax.fori_loop(0, (nc + wide - 1) // wide, col_step, 0)
    store = pltpu.make_async_copy(acc, out, acc_sem.at[1])
    store.start()
    store.wait()


def extend_add(parent, chunks, index_maps, place, per):
    count, split = len(chunks), len(chunks[0])
    rows, cols = parent.shape
    nrb, ncb = rows // BLK, cols // BLK
    depth = sum(chunk[0].shape[1] for chunk in chunks)
    even = 4 * BLK
    return pl.pallas_call(
        functools.partial(extend_body, count, per, split),
        grid_spec=pltpu.PrefetchScalarGridSpec(
            num_scalar_prefetch=2,
            grid=(1,),
            in_specs=[ANY] * (1 + count * split),
            out_specs=ANY,
            scratch_shapes=[
                pltpu.VMEM((rows, cols), F32),
                pltpu.VMEM((2, -(-rows // even) * even, depth), HALF),
                pltpu.VMEM((2, -(-cols // even) * even, depth), HALF),
                pltpu.SMEM((2, nrb + ncb + 2), jnp.int32),
                pltpu.SemaphoreType.DMA((2,)),
                pltpu.SemaphoreType.DMA((2,)),
            ],
        ),
        out_shape=jax.ShapeDtypeStruct((rows, cols), F32),
        compiler_params=pltpu.CompilerParams(vmem_limit_bytes=58 << 20),
        cost_estimate=pl.CostEstimate(
            flops=2 * rows * cols * depth, bytes_accessed=64 << 20, transcendentals=0
        ),
        name="extend_add",
    )(index_maps, place, parent, *[a for chunk in chunks for a in chunk])


def paired(size_grp, size_col, flip):
    route = []
    for g in range(size_grp):
        for c in range(size_col):
            to = flip(g, c)
            if to is not None:
                route.append((g * size_col + c, to[0] * size_col + to[1]))
    return route


def fronts_apart(diag_blocks, coupling, parent_front, index_maps):
    ng, nc = lax.axis_size("grp"), lax.axis_size("col")
    nz = nc // 2
    grp, col = lax.axis_index("grp"), lax.axis_index("col")
    width = diag_blocks.shape[1]
    blocks = coupling.shape[1] // width
    per = coupling.shape[0] // BLK

    def send(block, flip):
        return lax.ppermute(block, ("grp", "col"), paired(ng, nc, flip))

    def gather_rows(first, last):
        own = lax.slice_in_dim(diag_blocks, first * width, last * width, axis=0)
        along = [own]
        for dz in range(1, nz):
            along.append(send(own, lambda g, c: (g, c ^ 2 * dz) if c >= first else None))
        out = []
        for dz in range(nz):
            across = send(
                along[dz], lambda g, c: (g, c ^ 1) if c ^ 2 * dz >= first else None
            )
            out += [along[dz], across]
        return out

    cuts = [0, 1, 3, blocks]
    pieces = {}
    for first, last in zip(cuts, cuts[1:]):
        got = gather_rows(first, last)
        for k in range(first, last):
            pieces[k] = (first, got)

    col_id = jnp.reshape(col, (1,)).astype(jnp.int32)
    place = jnp.stack([grp, col, jnp.int32(nz)]).astype(jnp.int32)
    u_all = x_all = None
    chunks = []
    for k in range(blocks):
        first, got = pieces[k]
        u_all, x_all, half = factor_step(k, first, got, coupling, u_all, x_all, col_id)
        line = [half] + [send(half, lambda g, c: (g, c ^ 2 * dz)) for dz in range(1, nz)]
        own = jnp.concatenate(line, axis=0)

        def one_way(g, c):
            return (g ^ 2, c) if g % 2 == 0 else (g, c ^ 1)

        def other_way(g, c):
            return (g, c ^ 1) if g % 2 == 0 else (g ^ 2, c)

        side = send(own, one_way)
        here = [own, side, send(own, other_way), send(side, other_way)]
        there = [send(a, lambda g, c: (g ^ 1, c)) for a in here]
        chunks.append(here + there)

    merged = extend_add(parent_front, chunks, index_maps, place, per)
    mine = lax.dynamic_slice_in_dim(u_all, col * width, width, 0)
    return (merged, mine.T, x_all)


def on_device(diag_blocks, coupling, parent_front, index_maps):
    ng, nc = lax.axis_size("grp"), lax.axis_size("col")
    simple = (
        ng == FRONTS
        and nc % 2 == 0
        and nc & (nc - 1) == 0
        and diag_blocks.shape[1] == BLK
        and coupling.shape[0] % BLK == 0
    )
    body = fronts_apart if simple else general
    return body(diag_blocks, coupling, parent_front, index_maps)


def solution(mesh):
    in_specs = (P("grp", "col"), P(("grp", "col"), None), P("grp", "col"), P())
    out_specs = (P("grp", "col"), P("grp", "col"), P(("grp", "col"), None))
    return jax.shard_map(
        on_device, mesh=mesh, in_specs=in_specs, out_specs=out_specs, check_vma=False
    )
```

```python
import functools

import jax
import jax.numpy as jnp
from jax import lax
from jax.experimental import pallas as pl
from jax.experimental.pallas import tpu as pltpu
from jax.sharding import PartitionSpec as P

FRONTS = 4
BLK = 128
SBLK = 48
PBLK = 96
F32 = jnp.float32
HALF = jnp.bfloat16
EXACT = lax.Precision.HIGHEST
ANY = pl.BlockSpec(memory_space=pl.ANY)
PLAN = (1, 1, 2, 2, 2)


def swapped(block, axis, stride):
    count = lax.axis_size(axis)
    route = []
    for low in range(count):
        high = low | 1 << stride
        if high != low and high < count:
            route += [(low, high), (high, low)]
    return lax.ppermute(block, axis, route)


def place_rows(slab_blocks, source_block, present_count, count):
    picked = slab_blocks[jnp.arange(FRONTS)[:, None], source_block]
    picked = jnp.where(present_count[:, :, None, None] > 0, picked, jnp.zeros_like(picked))
    return jnp.transpose(picked, (1, 2, 0, 3)).reshape(count * BLK, -1)


def general(diag_blocks, coupling, parent_front, index_maps):
    groups = lax.axis_size("grp") // FRONTS
    swap_depth = groups.bit_length() - 1
    grp_index = lax.axis_index("grp")
    col_index = lax.axis_index("col")
    gathered = lax.all_gather(diag_blocks, "col", axis=1, tiled=True)
    for bit_pos in range(swap_depth):
        partner = swapped(gathered, "grp", bit_pos)
        is_upper = grp_index // 2**bit_pos % 2 == 1
        lower_half = jnp.where(is_upper, partner, gathered)
        upper_half = jnp.where(is_upper, gathered, partner)
        gathered = jnp.concatenate([lower_half, upper_half], axis=0)
    factor = jnp.linalg.cholesky(gathered)
    rows_here = diag_blocks.shape[0]
    col_width = diag_blocks.shape[1]
    local_start = grp_index % groups * rows_here
    factor_tile = lax.dynamic_slice(
        factor, (local_start, col_index * col_width), (rows_here, col_width)
    )
    panel_rows = lax.linalg.triangular_solve(
        factor, coupling, left_side=False, lower=True, transpose_a=True
    )
    panel_half = panel_rows.astype(HALF)
    panel_tiles = lax.all_to_all(panel_half, "col", split_axis=1, concat_axis=0, tiled=True)
    panel_slab = lax.all_gather(panel_tiles, "grp", axis=0, tiled=True)
    slab_blocks = panel_slab.reshape(FRONTS, SBLK, BLK, -1)
    parent_ids = jnp.arange(PBLK, dtype=jnp.int32)
    matches = (index_maps[:, :, None] == parent_ids[None, None, :]).astype(jnp.int32)
    present_count = jnp.sum(matches, axis=1)
    source_block = jnp.sum(matches * jnp.arange(SBLK, dtype=jnp.int32)[None, :, None], axis=1)
    row_count = parent_front.shape[0]
    contract = (((1,), (1,)), ((), ()))
    every_part = place_rows(slab_blocks, source_block, present_count, PBLK)
    col_operand = lax.all_to_all(every_part, "col", split_axis=0, concat_axis=1, tiled=True)
    row_part = lax.dynamic_slice_in_dim(every_part, grp_index * row_count, row_count, 0)
    update = lax.dot_general(
        lax.all_gather(row_part, "col", axis=1, tiled=True),
        col_operand,
        contract,
        preferred_element_type=F32,
    )
    return (parent_front - update, factor_tile, panel_rows)


def dot(a, b, ca, cb):
    return lax.dot_general(
        a, b, (((ca,), (cb,)), ((), ())), precision=EXACT, preferred_element_type=F32
    )


def eliminate(s_val, u_ref, inv_ref, width):
    rows = 8
    shape = (width, width)
    eye = lax.broadcasted_iota(jnp.int32, shape, 0) == lax.broadcasted_iota(jnp.int32, shape, 1)
    sub = lax.broadcasted_iota(jnp.int32, (rows, 1), 0)

    def group(g, carry):
        s, e = carry
        scale = jnp.zeros((rows, 1), F32)
        for i in range(rows):
            pivot = s[i : i + 1, i : i + 1]
            s_row, e_row = s[i : i + 1, :], e[i : i + 1, :]
            mult = s[:, i : i + 1] * (1.0 / pivot)
            below = jnp.where(sub > i, mult[:rows], 0.0)
            mult = jnp.concatenate([below, mult[rows:]], axis=0)
            s = s - mult * s_row
            e = e - mult * e_row
            scale = jnp.where(sub == i, lax.rsqrt(pivot), scale)
        at = pl.multiple_of(g * rows, rows)
        u_ref[pl.ds(at, rows), :] = pltpu.roll(s[:rows] * scale, at, 1)
        inv_ref[pl.ds(at, rows), :] = e[:rows] * scale
        s = jnp.concatenate([s[rows:], s[:rows]], axis=0)
        e = jnp.concatenate([e[rows:], e[:rows]], axis=0)
        return pltpu.roll(s, width - rows, 1), e

    lax.fori_loop(0, width // rows, group, (s_val, eye.astype(F32)))


def factor_body(k, width, cols, col_ref, *refs):
    pieces, c_ref, refs = refs[:cols], refs[cols], refs[cols + 1 :]
    if k:
        u_in, x_in, refs = refs[0], refs[1], refs[2:]
    u_out, x_out, half_ref, u_v, x_v, s_v, t_v, uk_v, inv_v, sem = refs
    n = s_v.shape[1]
    base = k * width
    rest = n - base - width
    here = pl.ds(base, width)
    if k:
        before = pl.ds(0, base)
        load_u = pltpu.make_async_copy(u_in.at[before, :], u_v.at[before, :], sem.at[0])
        load_x = pltpu.make_async_copy(x_in.at[:, before], x_v.at[:, before], sem.at[1])
        load_u.start()
        load_x.start()
    for rel in range(cols):
        at = pl.multiple_of((col_ref[0] ^ rel) * width, width)
        s_v[:, pl.ds(at, width)] = pieces[rel][...]
    if k:
        load_u.wait()

        def prev(j, _):
            at = pl.multiple_of(j * width, width)
            uj = u_v[pl.ds(at, width), pl.ds(base, n - base)]
            s_v[:, pl.ds(base, n - base)] -= dot(uj[:, :width], uj, 0, 0)
            return 0

        lax.fori_loop(0, k, prev, 0)
    eliminate(s_v[:, here], uk_v, inv_v, width)
    inv = inv_v[...]
    r = lax.broadcasted_iota(jnp.int32, (width, width), 0)
    c = lax.broadcasted_iota(jnp.int32, (width, width), 1)
    if base:
        u_v[here, pl.ds(0, base)] = jnp.zeros((width, base), F32)
    u_v[here, here] = jnp.where(c >= r, uk_v[...], 0.0)
    if rest:
        right = pl.ds(base + width, rest)
        u_v[here, right] = dot(inv, s_v[:, right], 1, 0)
    save_u = pltpu.make_async_copy(u_v.at[here, :], u_out.at[here, :], sem.at[2])
    save_u.start()
    t_v[...] = c_ref[...]
    if k:
        load_x.wait()

        def prevx(j, _):
            at = pl.multiple_of(j * width, width)
            t_v[...] -= dot(x_v[:, pl.ds(at, width)], u_v[pl.ds(at, width), here], 1, 0)
            return 0

        lax.fori_loop(0, k, prevx, 0)
    x_v[:, here] = dot(t_v[...], inv, 1, 1)
    half_ref[...] = x_v[:, here].astype(HALF)
    save_x = pltpu.make_async_copy(x_v.at[:, here], x_out.at[:, here], sem.at[3])
    save_x.start()
    save_u.wait()
    save_x.wait()


def factor_step(k, first, last, band, coupling, u_all, x_all, col_id):
    m, n = coupling.shape
    width = band[0].shape[1]
    cols = n // width
    args, specs = [], []
    for rel in range(cols):
        at = rel // 2 * (last - first) + k - first
        args.append(band[rel % 2])
        specs.append(pl.BlockSpec((width, width), lambda i, s, at=at: (at, 0)))
    args.append(coupling)
    specs += [pl.BlockSpec((m, width), lambda i, s: (0, k))]
    alias = {}
    if k:
        alias = {len(args) + 1: 0, len(args) + 2: 1}
        args += [u_all, x_all]
        specs += [ANY, ANY]
    square = pltpu.VMEM((width, width), F32)
    return pl.pallas_call(
        functools.partial(factor_body, k, width, cols),
        grid_spec=pltpu.PrefetchScalarGridSpec(
            num_scalar_prefetch=1,
            grid=(1,),
            in_specs=specs,
            out_specs=(ANY, ANY, pl.BlockSpec((m, width), lambda i, s: (0, 0))),
            scratch_shapes=[
                pltpu.VMEM((n, n), F32),
                pltpu.VMEM((m, n), F32),
                pltpu.VMEM((width, n), F32),
                pltpu.VMEM((m, width), F32),
                square,
                square,
                pltpu.SemaphoreType.DMA((4,)),
            ],
        ),
        out_shape=(
            jax.ShapeDtypeStruct((n, n), F32),
            jax.ShapeDtypeStruct((m, n), F32),
            jax.ShapeDtypeStruct((m, width), HALF),
        ),
        input_output_aliases=alias,
        compiler_params=pltpu.CompilerParams(vmem_limit_bytes=32 << 20),
        cost_estimate=pl.CostEstimate(
            flops=10**9, bytes_accessed=48 << 20, transcendentals=0
        ),
        name=f"factor{k}",
    )(col_id, *args)


def extend_body(count, per, split, maps, place, parent, *refs):
    arrays, refs = refs[: count * split], refs[count * split :]
    out, acc, lhs, rhs, lists, sem, acc_sem = refs
    rows, cols = parent.shape
    nrb, ncb = rows // BLK, cols // BLK
    widths = [arrays[n * split].shape[1] for n in range(count)]
    load = pltpu.make_async_copy(parent, acc, acc_sem.at[0])
    load.start()
    grp, col, zs = place[0], place[1], place[2]
    x_at, core_at = grp // 2, grp % 2

    def locate(f, i):
        src = i // per
        dc = (f % 2) ^ core_at
        dx = (f // 2) ^ x_at
        dcol = src ^ col
        dy = dcol % 2
        dz = dcol // 2
        near = jnp.where((core_at ^ dc) == 0, dx + 2 * dy, dy + 2 * dx)
        return 4 * dc + near, (dz * per + i % per) * BLK

    def fetch(f, slot):
        def scan(i, state):
            nr, nc = state
            p = maps[f, i]
            which, start = locate(f, i)
            start = pl.multiple_of(start, BLK)
            in_rows = p // nrb == grp
            in_cols = p // ncb == col

            @pl.when(in_rows)
            def _():
                lists[slot, nr] = p % nrb

            @pl.when(in_cols)
            def _():
                lists[slot, nrb + nc] = p % ncb

            @pl.when(in_rows | in_cols)
            def _():
                for a in range(split):

                    @pl.when(which == a)
                    def _():
                        for n in range(count):
                            src = arrays[n * split + a].at[pl.ds(start, BLK), :]
                            where = pl.ds(sum(widths[:n]), widths[n])

                            @pl.when(in_rows)
                            def _():
                                at = pl.ds(pl.multiple_of(nr * BLK, BLK), BLK)
                                pltpu.make_async_copy(
                                    src, lhs.at[slot, at, where], sem.at[slot]
                                ).start()

                            @pl.when(in_cols)
                            def _():
                                at = pl.ds(pl.multiple_of(nc * BLK, BLK), BLK)
                                pltpu.make_async_copy(
                                    src, rhs.at[slot, at, where], sem.at[slot]
                                ).start()

            return nr + in_rows.astype(jnp.int32), nc + in_cols.astype(jnp.int32)

        zero = jnp.int32(0)
        nr, nc = lax.fori_loop(0, maps.shape[1], scan, (zero, zero))
        lists[slot, nrb + ncb] = nr
        lists[slot, nrb + ncb + 1] = nc

    def drain(slot):
        total = lists[slot, nrb + ncb] + lists[slot, nrb + ncb + 1]

        def one(_, carry):
            block = lhs.at[slot, pl.ds(0, BLK), :]
            pltpu.make_async_copy(block, block, sem.at[slot]).wait()
            return carry

        lax.fori_loop(0, total, one, 0)

    fetch(0, 0)
    for f in range(FRONTS):
        slot = f % 2
        if f + 1 < FRONTS:
            fetch(f + 1, 1 - slot)
        drain(slot)
        if f == 0:
            load.wait()
        nr, nc = lists[slot, nrb + ncb], lists[slot, nrb + ncb + 1]
        tall, wide = 4, 2

        def col_step(j, _):
            right = rhs[slot, pl.ds(pl.multiple_of(j * wide * BLK, wide * BLK), wide * BLK), :]

            def row_step(i, _):
                left = lhs[slot, pl.ds(pl.multiple_of(i * tall * BLK, tall * BLK), tall * BLK), :]
                prod = lax.dot_general(
                    left, right, (((1,), (1,)), ((), ())), preferred_element_type=F32
                )
                for b in range(wide):
                    for a in range(tall):

                        @pl.when((i * tall + a < nr) & (j * wide + b < nc))
                        def _():
                            r = pl.multiple_of(lists[slot, i * tall + a] * BLK, BLK)
                            c = pl.multiple_of(lists[slot, nrb + j * wide + b] * BLK, BLK)
                            acc[pl.ds(r, BLK), pl.ds(c, BLK)] -= prod[
                                a * BLK : (a + 1) * BLK, b * BLK : (b + 1) * BLK
                            ]

                return 0

            lax.fori_loop(0, (nr + tall - 1) // tall, row_step, 0)
            return 0

        lax.fori_loop(0, (nc + wide - 1) // wide, col_step, 0)
    store = pltpu.make_async_copy(acc, out, acc_sem.at[1])
    store.start()
    store.wait()


def extend_add(parent, chunks, index_maps, place, per):
    count, split = len(chunks), len(chunks[0])
    rows, cols = parent.shape
    nrb, ncb = rows // BLK, cols // BLK
    depth = sum(chunk[0].shape[1] for chunk in chunks)
    even = 4 * BLK
    return pl.pallas_call(
        functools.partial(extend_body, count, per, split),
        grid_spec=pltpu.PrefetchScalarGridSpec(
            num_scalar_prefetch=2,
            grid=(1,),
            in_specs=[ANY] * (1 + count * split),
            out_specs=ANY,
            scratch_shapes=[
                pltpu.VMEM((rows, cols), F32),
                pltpu.VMEM((2, -(-rows // even) * even, depth), HALF),
                pltpu.VMEM((2, -(-cols // even) * even, depth), HALF),
                pltpu.SMEM((2, nrb + ncb + 2), jnp.int32),
                pltpu.SemaphoreType.DMA((2,)),
                pltpu.SemaphoreType.DMA((2,)),
            ],
        ),
        out_shape=jax.ShapeDtypeStruct((rows, cols), F32),
        compiler_params=pltpu.CompilerParams(vmem_limit_bytes=58 << 20),
        cost_estimate=pl.CostEstimate(
            flops=2 * rows * cols * depth, bytes_accessed=64 << 20, transcendentals=0
        ),
        name="extend_add",
    )(index_maps, place, parent, *[a for chunk in chunks for a in chunk])


def paired(size_grp, size_col, flip):
    route = []
    for g in range(size_grp):
        for c in range(size_col):
            to = flip(g, c)
            if to is not None:
                route.append((g * size_col + c, to[0] * size_col + to[1]))
    return route


def fronts_apart(diag_blocks, coupling, parent_front, index_maps):
    ng, nc = lax.axis_size("grp"), lax.axis_size("col")
    nz = nc // 2
    grp, col = lax.axis_index("grp"), lax.axis_index("col")
    width = diag_blocks.shape[1]
    blocks = coupling.shape[1] // width
    per = coupling.shape[0] // BLK

    def send(block, flip):
        return lax.ppermute(block, ("grp", "col"), paired(ng, nc, flip))

    def along_z(first, last):
        own = lax.slice_in_dim(diag_blocks, first * width, last * width, axis=0)
        pile = [own]
        for dz in range(1, nz):
            pile.append(send(own, lambda g, c: (g, c ^ 2 * dz) if c >= first else None))
        return pile

    def across_y(pile):
        near = jnp.concatenate(pile, axis=0)
        return near, send(near, lambda g, c: (g, c ^ 1))

    def one_way(g, c):
        return (g ^ 2, c) if g % 2 == 0 else (g, c ^ 1)

    def other_way(g, c):
        return (g, c ^ 1) if g % 2 == 0 else (g ^ 2, c)

    def other_core(g, c):
        return (g ^ 1, c)

    def advance(stage, held):
        if stage == 0:
            (half,) = held
            return [half] + [send(half, lambda g, c: (g, c ^ 2 * dz)) for dz in range(1, nz)]
        if stage == 1:
            own = jnp.concatenate(held, axis=0)
            return [own, send(own, one_way)]
        if stage == 2:
            return held + [send(a, other_way) for a in held]
        return held + [send(a, other_core) for a in held]

    cuts = [0, 1, 3, blocks]
    piles = [along_z(a, b) for a, b in zip(cuts[:2], cuts[1:3])]
    piles = lax.optimization_barrier(piles)
    bands = lax.optimization_barrier([across_y(piles[0])])
    band_of = {k: n for n, (a, b) in enumerate(zip(cuts, cuts[1:])) for k in range(a, b)}

    col_id = jnp.reshape(col, (1,)).astype(jnp.int32)
    place = jnp.stack([grp, col, jnp.int32(nz)]).astype(jnp.int32)
    u_all = x_all = None
    flying, done, stages = {}, {}, 4
    for slot in range(len(PLAN) + stages):
        for n in flying:
            if done[n] < stages:
                flying[n] = advance(done[n], flying[n])
                done[n] += 1
        if slot == 0:
            bands.append(across_y(piles[1]))
            piles = along_z(cuts[2], cuts[3])
        if slot == 1:
            bands.append(across_y(piles))
        if slot < len(PLAN):
            halves = []
            for k in range(sum(PLAN[:slot]), sum(PLAN[: slot + 1])):
                n = band_of[k]
                u_all, x_all, half = factor_step(
                    k, cuts[n], cuts[n + 1], bands[n], coupling, u_all, x_all, col_id
                )
                halves.append(half)
            flying[slot], done[slot] = [jnp.concatenate(halves, axis=1)], 0
        flying, piles, bands, u_all, x_all = lax.optimization_barrier(
            (flying, piles, bands, u_all, x_all)
        )
    chunks = [flying[n] for n in sorted(flying)]
    merged = extend_add(parent_front, chunks, index_maps, place, per)
    mine = lax.dynamic_slice_in_dim(u_all, col * width, width, 0)
    return (merged, mine.T, x_all)


def on_device(diag_blocks, coupling, parent_front, index_maps):
    ng, nc = lax.axis_size("grp"), lax.axis_size("col")
    simple = (
        ng == FRONTS
        and nc % 2 == 0
        and nc & (nc - 1) == 0
        and diag_blocks.shape[1] == BLK
        and coupling.shape[0] % BLK == 0
    )
    body = fronts_apart if simple else general
    return body(diag_blocks, coupling, parent_front, index_maps)


def solution(mesh):
    in_specs = (P("grp", "col"), P(("grp", "col"), None), P("grp", "col"), P())
    out_specs = (P("grp", "col"), P("grp", "col"), P(("grp", "col"), None))
    return jax.shard_map(
        on_device, mesh=mesh, in_specs=in_specs, out_specs=out_specs, check_vma=False
    )
```

```python
import functools

import jax
import jax.numpy as jnp
from jax import lax
from jax.experimental import pallas as pl
from jax.experimental.pallas import tpu as pltpu
from jax.sharding import PartitionSpec as P

FRONTS = 4
BLK = 128
SBLK = 48
PBLK = 96
F32 = jnp.float32
HALF = jnp.bfloat16
EXACT = lax.Precision.HIGHEST
ANY = pl.BlockSpec(memory_space=pl.ANY)


def swapped(block, axis, stride):
    count = lax.axis_size(axis)
    route = []
    for low in range(count):
        high = low | 1 << stride
        if high != low and high < count:
            route += [(low, high), (high, low)]
    return lax.ppermute(block, axis, route)


def place_rows(slab_blocks, source_block, present_count, count):
    picked = slab_blocks[jnp.arange(FRONTS)[:, None], source_block]
    picked = jnp.where(present_count[:, :, None, None] > 0, picked, jnp.zeros_like(picked))
    return jnp.transpose(picked, (1, 2, 0, 3)).reshape(count * BLK, -1)


def general(diag_blocks, coupling, parent_front, index_maps):
    groups = lax.axis_size("grp") // FRONTS
    swap_depth = groups.bit_length() - 1
    grp_index = lax.axis_index("grp")
    col_index = lax.axis_index("col")
    gathered = lax.all_gather(diag_blocks, "col", axis=1, tiled=True)
    for bit_pos in range(swap_depth):
        partner = swapped(gathered, "grp", bit_pos)
        is_upper = grp_index // 2**bit_pos % 2 == 1
        lower_half = jnp.where(is_upper, partner, gathered)
        upper_half = jnp.where(is_upper, gathered, partner)
        gathered = jnp.concatenate([lower_half, upper_half], axis=0)
    factor = jnp.linalg.cholesky(gathered)
    rows_here = diag_blocks.shape[0]
    col_width = diag_blocks.shape[1]
    local_start = grp_index % groups * rows_here
    factor_tile = lax.dynamic_slice(
        factor, (local_start, col_index * col_width), (rows_here, col_width)
    )
    panel_rows = lax.linalg.triangular_solve(
        factor, coupling, left_side=False, lower=True, transpose_a=True
    )
    panel_half = panel_rows.astype(HALF)
    panel_tiles = lax.all_to_all(panel_half, "col", split_axis=1, concat_axis=0, tiled=True)
    panel_slab = lax.all_gather(panel_tiles, "grp", axis=0, tiled=True)
    slab_blocks = panel_slab.reshape(FRONTS, SBLK, BLK, -1)
    parent_ids = jnp.arange(PBLK, dtype=jnp.int32)
    matches = (index_maps[:, :, None] == parent_ids[None, None, :]).astype(jnp.int32)
    present_count = jnp.sum(matches, axis=1)
    source_block = jnp.sum(matches * jnp.arange(SBLK, dtype=jnp.int32)[None, :, None], axis=1)
    row_count = parent_front.shape[0]
    contract = (((1,), (1,)), ((), ()))
    every_part = place_rows(slab_blocks, source_block, present_count, PBLK)
    col_operand = lax.all_to_all(every_part, "col", split_axis=0, concat_axis=1, tiled=True)
    row_part = lax.dynamic_slice_in_dim(every_part, grp_index * row_count, row_count, 0)
    update = lax.dot_general(
        lax.all_gather(row_part, "col", axis=1, tiled=True),
        col_operand,
        contract,
        preferred_element_type=F32,
    )
    return (parent_front - update, factor_tile, panel_rows)


def dot(a, b, ca, cb):
    return lax.dot_general(
        a, b, (((ca,), (cb,)), ((), ())), precision=EXACT, preferred_element_type=F32
    )


def eliminate(s_val, u_ref, inv_ref, width):
    rows = 8
    shape = (width, width)
    eye = lax.broadcasted_iota(jnp.int32, shape, 0) == lax.broadcasted_iota(jnp.int32, shape, 1)
    sub = lax.broadcasted_iota(jnp.int32, (rows, 1), 0)

    def group(g, carry):
        s, e = carry
        scale = jnp.zeros((rows, 1), F32)
        for i in range(rows):
            pivot = s[i : i + 1, i : i + 1]
            s_row, e_row = s[i : i + 1, :], e[i : i + 1, :]
            mult = s[:, i : i + 1] * (1.0 / pivot)
            below = jnp.where(sub > i, mult[:rows], 0.0)
            mult = jnp.concatenate([below, mult[rows:]], axis=0)
            s = s - mult * s_row
            e = e - mult * e_row
            scale = jnp.where(sub == i, lax.rsqrt(pivot), scale)
        at = pl.multiple_of(g * rows, rows)
        u_ref[pl.ds(at, rows), :] = pltpu.roll(s[:rows] * scale, at, 1)
        inv_ref[pl.ds(at, rows), :] = e[:rows] * scale
        s = jnp.concatenate([s[rows:], s[:rows]], axis=0)
        e = jnp.concatenate([e[rows:], e[:rows]], axis=0)
        return pltpu.roll(s, width - rows, 1), e

    lax.fori_loop(0, width // rows, group, (s_val, eye.astype(F32)))


def factor_body(k, width, cols, col_ref, *refs):
    pieces, c_ref, refs = refs[:cols], refs[cols], refs[cols + 1 :]
    if k:
        u_in, x_in, refs = refs[0], refs[1], refs[2:]
    u_out, x_out, half_ref, u_v, x_v, s_v, t_v, uk_v, inv_v, sem = refs
    n = s_v.shape[1]
    base = k * width
    rest = n - base - width
    here = pl.ds(base, width)
    if k:
        before = pl.ds(0, base)
        load_u = pltpu.make_async_copy(u_in.at[before, :], u_v.at[before, :], sem.at[0])
        load_x = pltpu.make_async_copy(x_in.at[:, before], x_v.at[:, before], sem.at[1])
        load_u.start()
        load_x.start()
    for rel in range(cols):
        at = pl.multiple_of((col_ref[0] ^ rel) * width, width)
        s_v[:, pl.ds(at, width)] = pieces[rel][...]
    if k:
        load_u.wait()

        def prev(j, _):
            at = pl.multiple_of(j * width, width)
            uj = u_v[pl.ds(at, width), pl.ds(base, n - base)]
            s_v[:, pl.ds(base, n - base)] -= dot(uj[:, :width], uj, 0, 0)
            return 0

        lax.fori_loop(0, k, prev, 0)
    eliminate(s_v[:, here], uk_v, inv_v, width)
    inv = inv_v[...]
    r = lax.broadcasted_iota(jnp.int32, (width, width), 0)
    c = lax.broadcasted_iota(jnp.int32, (width, width), 1)
    if base:
        u_v[here, pl.ds(0, base)] = jnp.zeros((width, base), F32)
    u_v[here, here] = jnp.where(c >= r, uk_v[...], 0.0)
    if rest:
        right = pl.ds(base + width, rest)
        u_v[here, right] = dot(inv, s_v[:, right], 1, 0)
    save_u = pltpu.make_async_copy(u_v.at[here, :], u_out.at[here, :], sem.at[2])
    save_u.start()
    t_v[...] = c_ref[...]
    if k:
        load_x.wait()

        def prevx(j, _):
            at = pl.multiple_of(j * width, width)
            t_v[...] -= dot(x_v[:, pl.ds(at, width)], u_v[pl.ds(at, width), here], 1, 0)
            return 0

        lax.fori_loop(0, k, prevx, 0)
    x_v[:, here] = dot(t_v[...], inv, 1, 1)
    half_ref[...] = x_v[:, here].astype(HALF)
    save_x = pltpu.make_async_copy(x_v.at[:, here], x_out.at[:, here], sem.at[3])
    save_x.start()
    save_u.wait()
    save_x.wait()


def factor_step(k, first, last, band, coupling, u_all, x_all, col_id):
    m, n = coupling.shape
    width = band[0].shape[1]
    cols = n // width
    args, specs = [], []
    for rel in range(cols):
        at = rel // 2 * (last - first) + k - first
        args.append(band[rel % 2])
        specs.append(pl.BlockSpec((width, width), lambda i, s, at=at: (at, 0)))
    args.append(coupling)
    specs += [pl.BlockSpec((m, width), lambda i, s: (0, k))]
    alias = {}
    if k:
        alias = {len(args) + 1: 0, len(args) + 2: 1}
        args += [u_all, x_all]
        specs += [ANY, ANY]
    square = pltpu.VMEM((width, width), F32)
    return pl.pallas_call(
        functools.partial(factor_body, k, width, cols),
        grid_spec=pltpu.PrefetchScalarGridSpec(
            num_scalar_prefetch=1,
            grid=(1,),
            in_specs=specs,
            out_specs=(ANY, ANY, pl.BlockSpec((m, width), lambda i, s: (0, 0))),
            scratch_shapes=[
                pltpu.VMEM((n, n), F32),
                pltpu.VMEM((m, n), F32),
                pltpu.VMEM((width, n), F32),
                pltpu.VMEM((m, width), F32),
                square,
                square,
                pltpu.SemaphoreType.DMA((4,)),
            ],
        ),
        out_shape=(
            jax.ShapeDtypeStruct((n, n), F32),
            jax.ShapeDtypeStruct((m, n), F32),
            jax.ShapeDtypeStruct((m, width), HALF),
        ),
        input_output_aliases=alias,
        compiler_params=pltpu.CompilerParams(vmem_limit_bytes=32 << 20),
        cost_estimate=pl.CostEstimate(
            flops=10**9, bytes_accessed=48 << 20, transcendentals=0
        ),
        name=f"factor{k}",
    )(col_id, *args)


def table_body(per, stride, span, nrb, ncb, maps, place, table):
    grp, col = place[0], place[1]
    x_at, core_at = grp // 2, grp % 2

    def front(f, _):
        base = f * stride

        def scan(i, state):
            nr, nc = state
            p = maps[f, i]
            dc = (f % 2) ^ core_at
            dx = (f // 2) ^ x_at
            dcol = (i // per) ^ col
            dy, dz = dcol % 2, dcol // 2
            near = jnp.where(f % 2 == 0, dx + 2 * dy, dy + 2 * dx)
            code = (4 * dc + near) * span + (dz * per + i % per)
            in_rows = p // nrb == grp
            in_cols = p // ncb == col

            @pl.when(in_rows)
            def _():
                table[base + 2 + 2 * nr] = p % nrb
                table[base + 3 + 2 * nr] = code

            @pl.when(in_cols)
            def _():
                table[base + 2 + 2 * (nrb + nc)] = p % ncb
                table[base + 3 + 2 * (nrb + nc)] = code

            return nr + in_rows.astype(jnp.int32), nc + in_cols.astype(jnp.int32)

        zero = jnp.int32(0)
        nr, nc = lax.fori_loop(0, maps.shape[1], scan, (zero, zero))
        table[base] = nr
        table[base + 1] = nc
        return 0

    lax.fori_loop(0, maps.shape[0], front, 0)


def block_table(index_maps, place, per, span, rows, cols):
    nrb, ncb = rows // BLK, cols // BLK
    stride = 2 * (1 + nrb + ncb)
    smem = pl.BlockSpec(memory_space=pltpu.SMEM)
    return pl.pallas_call(
        functools.partial(table_body, per, stride, span, nrb, ncb),
        in_specs=[smem, smem],
        out_specs=smem,
        out_shape=jax.ShapeDtypeStruct((FRONTS * stride,), jnp.int32),
        name="block_table",
    )(index_maps, place)


def extend_body(count, split, span, table, parent, *refs):
    arrays, refs = refs[: count * split], refs[count * split :]
    out, acc, lhs, rhs, sem, acc_sem = refs
    rows, cols = parent.shape
    nrb, ncb = rows // BLK, cols // BLK
    stride = 2 * (1 + nrb + ncb)
    widths = [arrays[n * split].shape[1] for n in range(count)]
    load = pltpu.make_async_copy(parent, acc, acc_sem.at[0])
    load.start()

    def fetch(f, slot):
        def bring(first, total, dst):
            def one(i, _):
                code = table[f * stride + 3 + 2 * (first + i)]
                start = pl.multiple_of(code % span * BLK, BLK)
                at = pl.ds(pl.multiple_of(i * BLK, BLK), BLK)
                for a in range(split):

                    @pl.when(code // span == a)
                    def _():
                        for n in range(count):
                            where = pl.ds(sum(widths[:n]), widths[n])
                            pltpu.make_async_copy(
                                arrays[n * split + a].at[pl.ds(start, BLK), :],
                                dst.at[slot, at, where],
                                sem.at[slot],
                            ).start()

                return 0

            lax.fori_loop(0, total, one, 0)

        bring(0, table[f * stride], lhs)
        bring(nrb, table[f * stride + 1], rhs)

    def drain(f, slot):
        def one(_, carry):
            block = lhs.at[slot, pl.ds(0, BLK), :]
            pltpu.make_async_copy(block, block, sem.at[slot]).wait()
            return carry

        lax.fori_loop(0, table[f * stride] + table[f * stride + 1], one, 0)

    fetch(0, 0)
    for f in range(FRONTS):
        slot = f % 2
        if f + 1 < FRONTS:
            fetch(f + 1, 1 - slot)
        drain(f, slot)
        if f == 0:
            load.wait()
        nr, nc = table[f * stride], table[f * stride + 1]
        tall, wide = 4, 4

        def col_step(j, _):
            right = rhs[slot, pl.ds(pl.multiple_of(j * wide * BLK, wide * BLK), wide * BLK), :]

            def row_step(i, _):
                left = lhs[slot, pl.ds(pl.multiple_of(i * tall * BLK, tall * BLK), tall * BLK), :]
                prod = lax.dot_general(
                    left, right, (((1,), (1,)), ((), ())), preferred_element_type=F32
                )
                for b in range(wide):
                    for a in range(tall):

                        @pl.when((i * tall + a < nr) & (j * wide + b < nc))
                        def _():
                            r = table[f * stride + 2 + 2 * (i * tall + a)]
                            c = table[f * stride + 2 + 2 * (nrb + j * wide + b)]
                            r = pl.multiple_of(r * BLK, BLK)
                            c = pl.multiple_of(c * BLK, BLK)
                            acc[pl.ds(r, BLK), pl.ds(c, BLK)] -= prod[
                                a * BLK : (a + 1) * BLK, b * BLK : (b + 1) * BLK
                            ]

                return 0

            lax.fori_loop(0, (nr + tall - 1) // tall, row_step, 0)
            return 0

        lax.fori_loop(0, (nc + wide - 1) // wide, col_step, 0)
    store = pltpu.make_async_copy(acc, out, acc_sem.at[1])
    store.start()
    store.wait()


def extend_add(parent, chunks, table, span, reuse):
    count, split = len(chunks), len(chunks[0])
    rows, cols = parent.shape
    depth = sum(chunk[0].shape[1] for chunk in chunks)
    even = 4 * BLK
    return pl.pallas_call(
        functools.partial(extend_body, count, split, span),
        grid_spec=pltpu.PrefetchScalarGridSpec(
            num_scalar_prefetch=1,
            grid=(1,),
            in_specs=[ANY] * (1 + count * split),
            out_specs=ANY,
            scratch_shapes=[
                pltpu.VMEM((rows, cols), F32),
                pltpu.VMEM((2, -(-rows // even) * even, depth), HALF),
                pltpu.VMEM((2, -(-cols // even) * even, depth), HALF),
                pltpu.SemaphoreType.DMA((2,)),
                pltpu.SemaphoreType.DMA((2,)),
            ],
        ),
        out_shape=jax.ShapeDtypeStruct((rows, cols), F32),
        input_output_aliases={1: 0} if reuse else {},
        compiler_params=pltpu.CompilerParams(
            vmem_limit_bytes=rows * cols * 4 + 4 * (rows + cols + even) * depth + (6 << 20)
        ),
        cost_estimate=pl.CostEstimate(
            flops=2 * rows * cols * depth, bytes_accessed=64 << 20, transcendentals=0
        ),
        name="extend_add",
    )(table, parent, *[a for chunk in chunks for a in chunk])


def paired(size_grp, size_col, flip):
    route = []
    for g in range(size_grp):
        for c in range(size_col):
            to = flip(g, c)
            if to is not None:
                route.append((g * size_col + c, to[0] * size_col + to[1]))
    return route


def fronts_apart(diag_blocks, coupling, parent_front, index_maps):
    ng, nc = lax.axis_size("grp"), lax.axis_size("col")
    nz = nc // 2
    grp, col = lax.axis_index("grp"), lax.axis_index("col")
    width = diag_blocks.shape[1]
    blocks = coupling.shape[1] // width
    per = coupling.shape[0] // BLK

    def send(block, flip):
        return lax.ppermute(block, ("grp", "col"), paired(ng, nc, flip))

    def along_z(first, last):
        own = lax.slice_in_dim(diag_blocks, first * width, last * width, axis=0)
        pile = [own]
        for dz in range(1, nz):
            pile.append(send(own, lambda g, c: (g, c ^ 2 * dz) if c >= first else None))
        return pile

    def across_y(pile):
        near = jnp.concatenate(pile, axis=0)
        return near, send(near, lambda g, c: (g, c ^ 1))

    def one_way(g, c):
        return (g ^ 2, c) if g % 2 == 0 else (g, c ^ 1)

    def other_way(g, c):
        return (g, c ^ 1) if g % 2 == 0 else (g ^ 2, c)

    def other_core(g, c):
        return (g ^ 1, c)

    def advance(stage, held):
        if stage == 0:
            (half,) = held
            return [half] + [send(half, lambda g, c: (g, c ^ 2 * dz)) for dz in range(1, nz)]
        if stage == 1:
            own = jnp.concatenate(held, axis=0)
            return [own, send(own, one_way)]
        if stage == 2:
            return held + [send(a, other_way) for a in held]
        return held + [send(a, other_core) for a in held]

    cuts = [0]
    while cuts[-1] < blocks:
        cuts.append(min(blocks, max(1, 2 * cuts[-1])))
    spans = list(zip(cuts, cuts[1:]))
    place = jnp.stack([grp, col]).astype(jnp.int32)
    span = nz * per
    table = block_table(index_maps, place, per, span, *parent_front.shape)
    piles, place, table = lax.optimization_barrier((along_z(*spans[0]), place, table))
    bands = [across_y(piles)]
    piles = along_z(*spans[1])
    piles, bands = lax.optimization_barrier((piles, bands))
    band_of = {k: n for n, (a, b) in enumerate(spans) for k in range(a, b)}

    col_id = place[1:]
    u_all = x_all = None
    merged = parent_front
    flying, done, stages = {}, {}, 4
    added = 0
    for slot in range(blocks + stages):
        for n in flying:
            if done[n] < stages:
                flying[n] = advance(done[n], flying[n])
                done[n] += 1
        if slot + 1 < len(spans):
            bands.append(across_y(piles))
            piles = along_z(*spans[slot + 2]) if slot + 2 < len(spans) else []
        if slot < blocks:
            n = band_of[slot]
            u_all, x_all, half = factor_step(
                slot, *spans[n], bands[n], coupling, u_all, x_all, col_id
            )
            flying[slot], done[slot] = [half], 0
        if slot == blocks:
            ready = range(added, blocks - stages)
            merged = extend_add(merged, [flying[n] for n in ready], table, span, added > 0)
            added = ready.stop
        flying, piles, bands, u_all, x_all, merged = lax.optimization_barrier(
            (flying, piles, bands, u_all, x_all, merged)
        )
    chunks = [flying[n] for n in range(added, blocks)]
    merged = extend_add(merged, chunks, table, span, added > 0)
    mine = lax.dynamic_slice_in_dim(u_all, col * width, width, 0)
    return (merged, mine.T, x_all)


def on_device(diag_blocks, coupling, parent_front, index_maps):
    ng, nc = lax.axis_size("grp"), lax.axis_size("col")
    simple = (
        ng == FRONTS
        and nc % 2 == 0
        and nc & (nc - 1) == 0
        and diag_blocks.shape[1] == BLK
        and coupling.shape[0] % BLK == 0
    )
    body = fronts_apart if simple else general
    return body(diag_blocks, coupling, parent_front, index_maps)


def solution(mesh):
    in_specs = (P("grp", "col"), P(("grp", "col"), None), P("grp", "col"), P())
    out_specs = (P("grp", "col"), P("grp", "col"), P(("grp", "col"), None))
    return jax.shard_map(
        on_device, mesh=mesh, in_specs=in_specs, out_specs=out_specs, check_vma=False
    )
```

```python
import functools

import jax
import jax.numpy as jnp
from jax import lax
from jax.experimental import pallas as pl
from jax.experimental.pallas import tpu as pltpu
from jax.sharding import PartitionSpec as P

FRONTS = 4
BLK = 128
SBLK = 48
PBLK = 96
F32 = jnp.float32
HALF = jnp.bfloat16
EXACT = lax.Precision.HIGHEST
HBM = pl.BlockSpec(memory_space=pltpu.HBM)


def swapped(block, axis, stride):
    count = lax.axis_size(axis)
    route = []
    for low in range(count):
        high = low | 1 << stride
        if high != low and high < count:
            route += [(low, high), (high, low)]
    return lax.ppermute(block, axis, route)


def place_rows(slab_blocks, source_block, present_count, count):
    picked = slab_blocks[jnp.arange(FRONTS)[:, None], source_block]
    picked = jnp.where(present_count[:, :, None, None] > 0, picked, jnp.zeros_like(picked))
    return jnp.transpose(picked, (1, 2, 0, 3)).reshape(count * BLK, -1)


def general(diag_blocks, coupling, parent_front, index_maps):
    groups = lax.axis_size("grp") // FRONTS
    swap_depth = groups.bit_length() - 1
    grp_index = lax.axis_index("grp")
    col_index = lax.axis_index("col")
    gathered = lax.all_gather(diag_blocks, "col", axis=1, tiled=True)
    for bit_pos in range(swap_depth):
        partner = swapped(gathered, "grp", bit_pos)
        is_upper = grp_index // 2**bit_pos % 2 == 1
        lower_half = jnp.where(is_upper, partner, gathered)
        upper_half = jnp.where(is_upper, gathered, partner)
        gathered = jnp.concatenate([lower_half, upper_half], axis=0)
    factor = jnp.linalg.cholesky(gathered)
    rows_here = diag_blocks.shape[0]
    col_width = diag_blocks.shape[1]
    local_start = grp_index % groups * rows_here
    factor_tile = lax.dynamic_slice(
        factor, (local_start, col_index * col_width), (rows_here, col_width)
    )
    panel_rows = lax.linalg.triangular_solve(
        factor, coupling, left_side=False, lower=True, transpose_a=True
    )
    panel_half = panel_rows.astype(HALF)
    panel_tiles = lax.all_to_all(panel_half, "col", split_axis=1, concat_axis=0, tiled=True)
    panel_slab = lax.all_gather(panel_tiles, "grp", axis=0, tiled=True)
    slab_blocks = panel_slab.reshape(FRONTS, SBLK, BLK, -1)
    parent_ids = jnp.arange(PBLK, dtype=jnp.int32)
    matches = (index_maps[:, :, None] == parent_ids[None, None, :]).astype(jnp.int32)
    present_count = jnp.sum(matches, axis=1)
    source_block = jnp.sum(matches * jnp.arange(SBLK, dtype=jnp.int32)[None, :, None], axis=1)
    row_count = parent_front.shape[0]
    contract = (((1,), (1,)), ((), ()))
    every_part = place_rows(slab_blocks, source_block, present_count, PBLK)
    col_operand = lax.all_to_all(every_part, "col", split_axis=0, concat_axis=1, tiled=True)
    row_part = lax.dynamic_slice_in_dim(every_part, grp_index * row_count, row_count, 0)
    update = lax.dot_general(
        lax.all_gather(row_part, "col", axis=1, tiled=True),
        col_operand,
        contract,
        preferred_element_type=F32,
    )
    return (parent_front - update, factor_tile, panel_rows)


def dot(a, b, ca, cb):
    return lax.dot_general(
        a, b, (((ca,), (cb,)), ((), ())), precision=EXACT, preferred_element_type=F32
    )


def eliminate(s_val, u_ref, inv_ref, width):
    rows = 8
    shape = (width, width)
    eye = lax.broadcasted_iota(jnp.int32, shape, 0) == lax.broadcasted_iota(jnp.int32, shape, 1)
    sub = lax.broadcasted_iota(jnp.int32, (rows, width), 0)

    def group(g, carry):
        s, e = carry
        top_s, top_e = s[:rows], e[:rows]
        cols = [jnp.broadcast_to(top_s[:, i : i + 1], (rows, width)) for i in range(rows)]
        u_s = jnp.zeros_like(top_s)
        u_e = jnp.zeros_like(top_e)
        for i in range(rows):
            me = sub == i
            root = lax.rsqrt(cols[i][i : i + 1, :])
            inv = root * root
            u_s = jnp.where(me, top_s * root, u_s)
            u_e = jnp.where(me, top_e * root, u_e)
            for j in range(i + 1, rows):
                w = cols[j][i : i + 1, :] * inv
                cols[j] = jnp.where(me, w, cols[j] - cols[i] * w)
            w_s = top_s[i : i + 1, :] * inv
            w_e = top_e[i : i + 1, :] * inv
            top_s = jnp.where(me, w_s, top_s - cols[i] * w_s)
            top_e = jnp.where(me, w_e, top_e - cols[i] * w_e)
        rest_s, rest_e = s[rows:], e[rows:]
        heads = [rest_s[:, i : i + 1] for i in range(rows)]
        for i in range(rows):
            rest_s = rest_s - heads[i] * top_s[i : i + 1, :]
            rest_e = rest_e - heads[i] * top_e[i : i + 1, :]
        at = pl.multiple_of(g * rows, rows)
        u_ref[pl.ds(at, rows), :] = pltpu.roll(u_s, at, 1)
        inv_ref[pl.ds(at, rows), :] = u_e
        s = jnp.concatenate([rest_s, s[:rows]], axis=0)
        e = jnp.concatenate([rest_e, e[:rows]], axis=0)
        return pltpu.roll(s, width - rows, 1), e

    lax.fori_loop(0, width // rows, group, (s_val, eye.astype(F32)))


def factor_body(k, width, cols, col_ref, *refs):
    pieces, c_ref, refs = refs[:cols], refs[cols], refs[cols + 1 :]
    if k:
        u_in, x_in, refs = refs[0], refs[1], refs[2:]
    u_out, x_out, half_ref, u_v, x_v, s_v, t_v, uk_v, inv_v, sem = refs
    n = s_v.shape[1]
    base = k * width
    rest = n - base - width
    here = pl.ds(base, width)
    if k:
        before = pl.ds(0, base)
        load_u = pltpu.make_async_copy(u_in.at[before, :], u_v.at[before, :], sem.at[0])
        load_x = pltpu.make_async_copy(x_in.at[:, before], x_v.at[:, before], sem.at[1])
        load_u.start()
        load_x.start()
    for rel in range(cols):
        at = pl.multiple_of((col_ref[0] ^ rel) * width, width)
        s_v[:, pl.ds(at, width)] = pieces[rel][...]
    if k:
        load_u.wait()

        def prev(j, _):
            at = pl.multiple_of(j * width, width)
            uj = u_v[pl.ds(at, width), pl.ds(base, n - base)]
            s_v[:, pl.ds(base, n - base)] -= dot(uj[:, :width], uj, 0, 0)
            return 0

        lax.fori_loop(0, k, prev, 0)
    eliminate(s_v[:, here], uk_v, inv_v, width)
    inv = inv_v[...]
    r = lax.broadcasted_iota(jnp.int32, (width, width), 0)
    c = lax.broadcasted_iota(jnp.int32, (width, width), 1)
    if base:
        u_v[here, pl.ds(0, base)] = jnp.zeros((width, base), F32)
    u_v[here, here] = jnp.where(c >= r, uk_v[...], 0.0)
    if rest:
        right = pl.ds(base + width, rest)
        u_v[here, right] = dot(inv, s_v[:, right], 1, 0)
    save_u = pltpu.make_async_copy(u_v.at[here, :], u_out.at[here, :], sem.at[2])
    save_u.start()
    t_v[...] = c_ref[...]
    if k:
        load_x.wait()

        def prevx(j, _):
            at = pl.multiple_of(j * width, width)
            t_v[...] -= dot(x_v[:, pl.ds(at, width)], u_v[pl.ds(at, width), here], 1, 0)
            return 0

        lax.fori_loop(0, k, prevx, 0)
    x_v[:, here] = dot(t_v[...], inv, 1, 1)
    half_ref[...] = x_v[:, here].astype(HALF)
    save_x = pltpu.make_async_copy(x_v.at[:, here], x_out.at[:, here], sem.at[3])
    save_x.start()
    save_u.wait()
    save_x.wait()


def factor_step(k, first, last, band, coupling, u_all, x_all, col_id):
    m, n = coupling.shape
    width = band[0].shape[1]
    cols = n // width
    args, specs = [], []
    for rel in range(cols):
        at = rel // 2 * (last - first) + k - first
        args.append(band[rel % 2])
        specs.append(pl.BlockSpec((width, width), lambda i, s, at=at: (at, 0)))
    args.append(coupling)
    specs += [pl.BlockSpec((m, width), lambda i, s: (0, k))]
    alias = {}
    if k:
        alias = {len(args) + 1: 0, len(args) + 2: 1}
        args += [u_all, x_all]
        specs += [HBM, HBM]
    square = pltpu.VMEM((width, width), F32)
    return pl.pallas_call(
        functools.partial(factor_body, k, width, cols),
        grid_spec=pltpu.PrefetchScalarGridSpec(
            num_scalar_prefetch=1,
            grid=(1,),
            in_specs=specs,
            out_specs=(HBM, HBM, pl.BlockSpec((m, width), lambda i, s: (0, 0))),
            scratch_shapes=[
                pltpu.VMEM((n, n), F32),
                pltpu.VMEM((m, n), F32),
                pltpu.VMEM((width, n), F32),
                pltpu.VMEM((m, width), F32),
                square,
                square,
                pltpu.SemaphoreType.DMA((4,)),
            ],
        ),
        out_shape=(
            jax.ShapeDtypeStruct((n, n), F32),
            jax.ShapeDtypeStruct((m, n), F32),
            jax.ShapeDtypeStruct((m, width), HALF),
        ),
        input_output_aliases=alias,
        compiler_params=pltpu.CompilerParams(vmem_limit_bytes=60 << 20),
        cost_estimate=pl.CostEstimate(
            flops=10**9, bytes_accessed=48 << 20, transcendentals=0
        ),
        name=f"factor{k}",
    )(col_id, *args)


def table_body(per, stride, span, nrb, ncb, maps, place, table):
    grp, col = place[0], place[1]
    x_at, core_at = grp // 2, grp % 2

    def front(f, _):
        base = f * stride

        def scan(i, state):
            nr, nc = state
            p = maps[f, i]
            dc = (f % 2) ^ core_at
            dx = (f // 2) ^ x_at
            dcol = (i // per) ^ col
            dy, dz = dcol % 2, dcol // 2
            near = jnp.where(f % 2 == 0, dx + 2 * dy, dy + 2 * dx)
            code = (4 * dc + near) * span + (dz * per + i % per)
            in_rows = p // nrb == grp
            in_cols = p // ncb == col

            @pl.when(in_rows)
            def _():
                table[base + 2 + 2 * nr] = p % nrb
                table[base + 3 + 2 * nr] = code

            @pl.when(in_cols)
            def _():
                table[base + 2 + 2 * (nrb + nc)] = p % ncb
                table[base + 3 + 2 * (nrb + nc)] = code

            return nr + in_rows.astype(jnp.int32), nc + in_cols.astype(jnp.int32)

        zero = jnp.int32(0)
        nr, nc = lax.fori_loop(0, maps.shape[1], scan, (zero, zero))
        table[base] = nr
        table[base + 1] = nc
        return 0

    lax.fori_loop(0, maps.shape[0], front, 0)


def block_table(index_maps, place, per, span, rows, cols):
    nrb, ncb = rows // BLK, cols // BLK
    stride = 2 * (1 + nrb + ncb)
    smem = pl.BlockSpec(memory_space=pltpu.SMEM)
    return pl.pallas_call(
        functools.partial(table_body, per, stride, span, nrb, ncb),
        in_specs=[smem, smem],
        out_specs=smem,
        out_shape=jax.ShapeDtypeStruct((FRONTS * stride,), jnp.int32),
        name="block_table",
    )(index_maps, place)


def extend_body(count, split, span, table, parent, *refs):
    arrays, refs = refs[: count * split], refs[count * split :]
    out, acc, lhs, rhs, sem, acc_sem = refs
    rows, cols = parent.shape
    nrb, ncb = rows // BLK, cols // BLK
    stride = 2 * (1 + nrb + ncb)
    widths = [arrays[n * split].shape[1] for n in range(count)]
    load = pltpu.make_async_copy(parent, acc, acc_sem.at[0])
    load.start()

    def fetch(f, slot):
        def bring(first, total, dst):
            def one(i, _):
                code = table[f * stride + 3 + 2 * (first + i)]
                start = pl.multiple_of(code % span * BLK, BLK)
                at = pl.ds(pl.multiple_of(i * BLK, BLK), BLK)
                for a in range(split):

                    @pl.when(code // span == a)
                    def _():
                        for n in range(count):
                            where = pl.ds(sum(widths[:n]), widths[n])
                            pltpu.make_async_copy(
                                arrays[n * split + a].at[pl.ds(start, BLK), :],
                                dst.at[slot, at, where],
                                sem.at[slot],
                            ).start()

                return 0

            lax.fori_loop(0, total, one, 0)

        bring(0, table[f * stride], lhs)
        bring(nrb, table[f * stride + 1], rhs)

    def drain(f, slot):
        def one(_, carry):
            block = lhs.at[slot, pl.ds(0, BLK), :]
            pltpu.make_async_copy(block, block, sem.at[slot]).wait()
            return carry

        lax.fori_loop(0, table[f * stride] + table[f * stride + 1], one, 0)

    fetch(0, 0)
    for f in range(FRONTS):
        slot = f % 2
        if f + 1 < FRONTS:
            fetch(f + 1, 1 - slot)
        drain(f, slot)
        if f == 0:
            load.wait()
        nr, nc = table[f * stride], table[f * stride + 1]
        tall, wide = 4, 4

        def col_step(j, _):
            right = rhs[slot, pl.ds(pl.multiple_of(j * wide * BLK, wide * BLK), wide * BLK), :]

            def row_step(i, _):
                left = lhs[slot, pl.ds(pl.multiple_of(i * tall * BLK, tall * BLK), tall * BLK), :]
                prod = lax.dot_general(
                    left, right, (((1,), (1,)), ((), ())), preferred_element_type=F32
                )
                for b in range(wide):
                    for a in range(tall):

                        @pl.when((i * tall + a < nr) & (j * wide + b < nc))
                        def _():
                            r = table[f * stride + 2 + 2 * (i * tall + a)]
                            c = table[f * stride + 2 + 2 * (nrb + j * wide + b)]
                            r = pl.multiple_of(r * BLK, BLK)
                            c = pl.multiple_of(c * BLK, BLK)
                            acc[pl.ds(r, BLK), pl.ds(c, BLK)] -= prod[
                                a * BLK : (a + 1) * BLK, b * BLK : (b + 1) * BLK
                            ]

                return 0

            lax.fori_loop(0, (nr + tall - 1) // tall, row_step, 0)
            return 0

        lax.fori_loop(0, (nc + wide - 1) // wide, col_step, 0)
    store = pltpu.make_async_copy(acc, out, acc_sem.at[1])
    store.start()
    store.wait()


def extend_add(parent, chunks, table, span, reuse):
    count, split = len(chunks), len(chunks[0])
    rows, cols = parent.shape
    depth = sum(chunk[0].shape[1] for chunk in chunks)
    even = 4 * BLK
    return pl.pallas_call(
        functools.partial(extend_body, count, split, span),
        grid_spec=pltpu.PrefetchScalarGridSpec(
            num_scalar_prefetch=1,
            grid=(1,),
            in_specs=[HBM] * (1 + count * split),
            out_specs=HBM,
            scratch_shapes=[
                pltpu.VMEM((rows, cols), F32),
                pltpu.VMEM((2, -(-rows // even) * even, depth), HALF),
                pltpu.VMEM((2, -(-cols // even) * even, depth), HALF),
                pltpu.SemaphoreType.DMA((2,)),
                pltpu.SemaphoreType.DMA((2,)),
            ],
        ),
        out_shape=jax.ShapeDtypeStruct((rows, cols), F32),
        input_output_aliases={1: 0} if reuse else {},
        compiler_params=pltpu.CompilerParams(vmem_limit_bytes=60 << 20),
        cost_estimate=pl.CostEstimate(
            flops=2 * rows * cols * depth, bytes_accessed=64 << 20, transcendentals=0
        ),
        name="extend_add",
    )(table, parent, *[a for chunk in chunks for a in chunk])


def paired(size_grp, size_col, flip):
    route = []
    for g in range(size_grp):
        for c in range(size_col):
            to = flip(g, c)
            if to is not None:
                route.append((g * size_col + c, to[0] * size_col + to[1]))
    return route


def fronts_apart(diag_blocks, coupling, parent_front, index_maps):
    ng, nc = lax.axis_size("grp"), lax.axis_size("col")
    nz = nc // 2
    grp, col = lax.axis_index("grp"), lax.axis_index("col")
    width = diag_blocks.shape[1]
    blocks = coupling.shape[1] // width
    per = coupling.shape[0] // BLK

    def send(block, flip):
        return lax.ppermute(block, ("grp", "col"), paired(ng, nc, flip))

    def along_z(first, last):
        own = lax.slice_in_dim(diag_blocks, first * width, last * width, axis=0)
        pile = [own]
        for dz in range(1, nz):
            pile.append(send(own, lambda g, c: (g, c ^ 2 * dz) if c >= first else None))
        return pile

    def across_y(pile):
        near = jnp.concatenate(pile, axis=0)
        return near, send(near, lambda g, c: (g, c ^ 1))

    def one_way(g, c):
        return (g ^ 2, c) if g % 2 == 0 else (g, c ^ 1)

    def other_way(g, c):
        return (g, c ^ 1) if g % 2 == 0 else (g ^ 2, c)

    def other_core(g, c):
        return (g ^ 1, c)

    def advance(stage, held):
        if stage == 0:
            (half,) = held
            return [half] + [send(half, lambda g, c: (g, c ^ 2 * dz)) for dz in range(1, nz)]
        if stage == 1:
            own = jnp.concatenate(held, axis=0)
            return [own, send(own, one_way)]
        if stage == 2:
            return held + [send(a, other_way) for a in held]
        return held + [send(a, other_core) for a in held]

    cuts = [0]
    while cuts[-1] < blocks:
        cuts.append(min(blocks, max(1, 2 * cuts[-1])))
    spans = list(zip(cuts, cuts[1:]))
    place = jnp.stack([grp, col]).astype(jnp.int32)
    span = nz * per
    table = block_table(index_maps, place, per, span, *parent_front.shape)
    piles, place, table = lax.optimization_barrier((along_z(*spans[0]), place, table))
    bands = [across_y(piles)]
    piles = along_z(*spans[1])
    piles, bands = lax.optimization_barrier((piles, bands))
    band_of = {k: n for n, (a, b) in enumerate(spans) for k in range(a, b)}

    col_id = place[1:]
    u_all = x_all = None
    merged = parent_front
    flying, done, stages = {}, {}, 4
    added = 0
    for slot in range(blocks + stages):
        for n in flying:
            if done[n] < stages:
                flying[n] = advance(done[n], flying[n])
                done[n] += 1
        if slot + 1 < len(spans):
            bands.append(across_y(piles))
            piles = along_z(*spans[slot + 2]) if slot + 2 < len(spans) else []
        if slot < blocks:
            n = band_of[slot]
            u_all, x_all, half = factor_step(
                slot, *spans[n], bands[n], coupling, u_all, x_all, col_id
            )
            flying[slot], done[slot] = [half], 0
        if slot == blocks:
            ready = range(added, blocks - stages)
            merged = extend_add(merged, [flying[n] for n in ready], table, span, added > 0)
            added = ready.stop
        flying, piles, bands, u_all, x_all, merged = lax.optimization_barrier(
            (flying, piles, bands, u_all, x_all, merged)
        )
    chunks = [flying[n] for n in range(added, blocks)]
    merged = extend_add(merged, chunks, table, span, added > 0)
    mine = lax.dynamic_slice_in_dim(u_all, col * width, width, 0)
    return (merged, mine.T, x_all)


def on_device(diag_blocks, coupling, parent_front, index_maps):
    ng, nc = lax.axis_size("grp"), lax.axis_size("col")
    simple = (
        ng == FRONTS
        and nc % 2 == 0
        and nc & (nc - 1) == 0
        and diag_blocks.shape[1] == BLK
        and coupling.shape[0] % BLK == 0
    )
    body = fronts_apart if simple else general
    return body(diag_blocks, coupling, parent_front, index_maps)


def solution(mesh):
    in_specs = (P("grp", "col"), P(("grp", "col"), None), P("grp", "col"), P())
    out_specs = (P("grp", "col"), P("grp", "col"), P(("grp", "col"), None))
    return jax.shard_map(
        on_device, mesh=mesh, in_specs=in_specs, out_specs=out_specs, check_vma=False
    )
```

```python
import functools

import jax
import jax.numpy as jnp
from jax import lax
from jax.experimental import pallas as pl
from jax.experimental.pallas import tpu as pltpu
from jax.sharding import PartitionSpec as P

FRONTS = 4
BLK = 128
SBLK = 48
PBLK = 96
F32 = jnp.float32
HALF = jnp.bfloat16
EXACT = lax.Precision.HIGHEST
HBM = pl.BlockSpec(memory_space=pltpu.HBM)


def swapped(block, axis, stride):
    count = lax.axis_size(axis)
    route = []
    for low in range(count):
        high = low | 1 << stride
        if high != low and high < count:
            route += [(low, high), (high, low)]
    return lax.ppermute(block, axis, route)


def place_rows(slab_blocks, source_block, present_count, count):
    picked = slab_blocks[jnp.arange(FRONTS)[:, None], source_block]
    picked = jnp.where(present_count[:, :, None, None] > 0, picked, jnp.zeros_like(picked))
    return jnp.transpose(picked, (1, 2, 0, 3)).reshape(count * BLK, -1)


def general(diag_blocks, coupling, parent_front, index_maps):
    groups = lax.axis_size("grp") // FRONTS
    swap_depth = groups.bit_length() - 1
    grp_index = lax.axis_index("grp")
    col_index = lax.axis_index("col")
    gathered = lax.all_gather(diag_blocks, "col", axis=1, tiled=True)
    for bit_pos in range(swap_depth):
        partner = swapped(gathered, "grp", bit_pos)
        is_upper = grp_index // 2**bit_pos % 2 == 1
        lower_half = jnp.where(is_upper, partner, gathered)
        upper_half = jnp.where(is_upper, gathered, partner)
        gathered = jnp.concatenate([lower_half, upper_half], axis=0)
    factor = jnp.linalg.cholesky(gathered)
    rows_here = diag_blocks.shape[0]
    col_width = diag_blocks.shape[1]
    local_start = grp_index % groups * rows_here
    factor_tile = lax.dynamic_slice(
        factor, (local_start, col_index * col_width), (rows_here, col_width)
    )
    panel_rows = lax.linalg.triangular_solve(
        factor, coupling, left_side=False, lower=True, transpose_a=True
    )
    panel_half = panel_rows.astype(HALF)
    panel_tiles = lax.all_to_all(panel_half, "col", split_axis=1, concat_axis=0, tiled=True)
    panel_slab = lax.all_gather(panel_tiles, "grp", axis=0, tiled=True)
    slab_blocks = panel_slab.reshape(FRONTS, SBLK, BLK, -1)
    parent_ids = jnp.arange(PBLK, dtype=jnp.int32)
    matches = (index_maps[:, :, None] == parent_ids[None, None, :]).astype(jnp.int32)
    present_count = jnp.sum(matches, axis=1)
    source_block = jnp.sum(matches * jnp.arange(SBLK, dtype=jnp.int32)[None, :, None], axis=1)
    row_count = parent_front.shape[0]
    contract = (((1,), (1,)), ((), ()))
    every_part = place_rows(slab_blocks, source_block, present_count, PBLK)
    col_operand = lax.all_to_all(every_part, "col", split_axis=0, concat_axis=1, tiled=True)
    row_part = lax.dynamic_slice_in_dim(every_part, grp_index * row_count, row_count, 0)
    update = lax.dot_general(
        lax.all_gather(row_part, "col", axis=1, tiled=True),
        col_operand,
        contract,
        preferred_element_type=F32,
    )
    return (parent_front - update, factor_tile, panel_rows)


def dot(a, b, ca, cb):
    return lax.dot_general(
        a, b, (((ca,), (cb,)), ((), ())), precision=EXACT, preferred_element_type=F32
    )


def eliminate(s_val, u_ref, inv_ref, width):
    rows = 8
    shape = (width, width)
    eye = lax.broadcasted_iota(jnp.int32, shape, 0) == lax.broadcasted_iota(jnp.int32, shape, 1)
    sub = lax.broadcasted_iota(jnp.int32, (rows, width), 0)

    def group(g, carry):
        s, e = carry
        top_s, top_e = s[:rows], e[:rows]
        cols = [jnp.broadcast_to(top_s[:, i : i + 1], (rows, width)) for i in range(rows)]
        u_s = jnp.zeros_like(top_s)
        u_e = jnp.zeros_like(top_e)
        for i in range(rows):
            me = sub == i
            root = lax.rsqrt(cols[i][i : i + 1, :])
            inv = root * root
            u_s = jnp.where(me, top_s * root, u_s)
            u_e = jnp.where(me, top_e * root, u_e)
            for j in range(i + 1, rows):
                w = cols[j][i : i + 1, :] * inv
                cols[j] = jnp.where(me, w, cols[j] - cols[i] * w)
            w_s = top_s[i : i + 1, :] * inv
            w_e = top_e[i : i + 1, :] * inv
            top_s = jnp.where(me, w_s, top_s - cols[i] * w_s)
            top_e = jnp.where(me, w_e, top_e - cols[i] * w_e)
        rest_s, rest_e = s[rows:], e[rows:]
        heads = [rest_s[:, i : i + 1] for i in range(rows)]
        for i in range(rows):
            rest_s = rest_s - heads[i] * top_s[i : i + 1, :]
            rest_e = rest_e - heads[i] * top_e[i : i + 1, :]
        at = pl.multiple_of(g * rows, rows)
        u_ref[pl.ds(at, rows), :] = pltpu.roll(u_s, at, 1)
        inv_ref[pl.ds(at, rows), :] = u_e
        s = jnp.concatenate([rest_s, s[:rows]], axis=0)
        e = jnp.concatenate([rest_e, e[:rows]], axis=0)
        return pltpu.roll(s, width - rows, 1), e

    lax.fori_loop(0, width // rows, group, (s_val, eye.astype(F32)))


def factor_body(k, width, cols, col_ref, *refs):
    pieces, c_ref, refs = refs[:cols], refs[cols], refs[cols + 1 :]
    if k:
        u_in, x_in, refs = refs[0], refs[1], refs[2:]
    u_out, x_out, half_ref, u_v, x_v, s_v, t_v, uk_v, inv_v, sem = refs
    n = s_v.shape[1]
    base = k * width
    rest = n - base - width
    here = pl.ds(base, width)
    if k:
        before = pl.ds(0, base)
        load_u = pltpu.make_async_copy(u_in.at[before, :], u_v.at[before, :], sem.at[0])
        load_x = pltpu.make_async_copy(x_in.at[:, before], x_v.at[:, before], sem.at[1])
        load_u.start()
        load_x.start()
    for rel in range(cols):
        at = pl.multiple_of((col_ref[0] ^ rel) * width, width)
        s_v[:, pl.ds(at, width)] = pieces[rel][...]
    if k:
        load_u.wait()

        def prev(j, _):
            at = pl.multiple_of(j * width, width)
            uj = u_v[pl.ds(at, width), pl.ds(base, n - base)]
            s_v[:, pl.ds(base, n - base)] -= dot(uj[:, :width], uj, 0, 0)
            return 0

        lax.fori_loop(0, k, prev, 0)
    eliminate(s_v[:, here], uk_v, inv_v, width)
    inv = inv_v[...]
    r = lax.broadcasted_iota(jnp.int32, (width, width), 0)
    c = lax.broadcasted_iota(jnp.int32, (width, width), 1)
    if base:
        u_v[here, pl.ds(0, base)] = jnp.zeros((width, base), F32)
    u_v[here, here] = jnp.where(c >= r, uk_v[...], 0.0)
    if rest:
        right = pl.ds(base + width, rest)
        u_v[here, right] = dot(inv, s_v[:, right], 1, 0)
    save_u = pltpu.make_async_copy(u_v.at[here, :], u_out.at[here, :], sem.at[2])
    save_u.start()
    t_v[...] = c_ref[...]
    if k:
        load_x.wait()

        def prevx(j, _):
            at = pl.multiple_of(j * width, width)
            t_v[...] -= dot(x_v[:, pl.ds(at, width)], u_v[pl.ds(at, width), here], 1, 0)
            return 0

        lax.fori_loop(0, k, prevx, 0)
    x_v[:, here] = dot(t_v[...], inv, 1, 1)
    half_ref[...] = x_v[:, here].astype(HALF)
    save_x = pltpu.make_async_copy(x_v.at[:, here], x_out.at[:, here], sem.at[3])
    save_x.start()
    save_u.wait()
    save_x.wait()


def factor_step(k, first, last, band, coupling, u_all, x_all, col_id):
    m, n = coupling.shape
    width = band[0].shape[1]
    cols = n // width
    args, specs = [], []
    for rel in range(cols):
        at = rel // 2 * (last - first) + k - first
        args.append(band[rel % 2])
        specs.append(pl.BlockSpec((width, width), lambda i, s, at=at: (at, 0)))
    args.append(coupling)
    specs += [pl.BlockSpec((m, width), lambda i, s: (0, k))]
    alias = {}
    if k:
        alias = {len(args) + 1: 0, len(args) + 2: 1}
        args += [u_all, x_all]
        specs += [HBM, HBM]
    square = pltpu.VMEM((width, width), F32)
    return pl.pallas_call(
        functools.partial(factor_body, k, width, cols),
        grid_spec=pltpu.PrefetchScalarGridSpec(
            num_scalar_prefetch=1,
            grid=(1,),
            in_specs=specs,
            out_specs=(HBM, HBM, pl.BlockSpec((m, width), lambda i, s: (0, 0))),
            scratch_shapes=[
                pltpu.VMEM((n, n), F32),
                pltpu.VMEM((m, n), F32),
                pltpu.VMEM((width, n), F32),
                pltpu.VMEM((m, width), F32),
                square,
                square,
                pltpu.SemaphoreType.DMA((4,)),
            ],
        ),
        out_shape=(
            jax.ShapeDtypeStruct((n, n), F32),
            jax.ShapeDtypeStruct((m, n), F32),
            jax.ShapeDtypeStruct((m, width), HALF),
        ),
        input_output_aliases=alias,
        compiler_params=pltpu.CompilerParams(vmem_limit_bytes=60 << 20),
        cost_estimate=pl.CostEstimate(
            flops=10**9, bytes_accessed=48 << 20, transcendentals=0
        ),
        name=f"factor{k}",
    )(col_id, *args)


def table_layout(rows, cols):
    nrb, ncb = rows // BLK, cols // BLK
    strips = next(n for n in (3, 2, 1) if nrb % n == 0)
    head = strips + 2
    return nrb, ncb, strips, head, head + 2 * (nrb + ncb)


def table_body(per, span, layout, maps, place, table, source):
    nrb, ncb, strips, head, stride = layout
    grp, col = place[0], place[1]
    x_at, core_at = grp // 2, grp % 2
    size = source.shape[0]

    def front(f, _):
        base = f * stride

        def clear(p, _):
            source[p] = -1
            return 0

        def mark(i, _):
            source[maps[f, i]] = i
            return 0

        lax.fori_loop(0, size, clear, 0)
        lax.fori_loop(0, maps.shape[1], mark, 0)

        def entry(where, p, i):
            dc = (f % 2) ^ core_at
            dx = (f // 2) ^ x_at
            dcol = (i // per) ^ col
            dy, dz = dcol % 2, dcol // 2
            near = jnp.where(f % 2 == 0, dx + 2 * dy, dy + 2 * dx)
            table[where] = p
            table[where + 1] = (4 * dc + near) * span + (dz * per + i % per)

        def row(p, n):
            i = source[grp * nrb + p]

            @pl.when(p % (nrb // strips) == 0)
            def _():
                table[base + 1 + p // (nrb // strips)] = n

            @pl.when(i >= 0)
            def _():
                entry(base + head + 2 * n, p, i)

            return n + (i >= 0).astype(jnp.int32)

        def column(p, n):
            i = source[col * ncb + p]

            @pl.when(i >= 0)
            def _():
                entry(base + head + 2 * (nrb + n), p, i)

            return n + (i >= 0).astype(jnp.int32)

        table[base + 1 + strips] = lax.fori_loop(0, nrb, row, jnp.int32(0))
        table[base] = lax.fori_loop(0, ncb, column, jnp.int32(0))
        return 0

    lax.fori_loop(0, maps.shape[0], front, 0)


def block_table(index_maps, place, per, span, size, shape):
    layout = table_layout(*shape)
    smem = pl.BlockSpec(memory_space=pltpu.SMEM)
    return pl.pallas_call(
        functools.partial(table_body, per, span, layout),
        in_specs=[smem, smem],
        out_specs=smem,
        out_shape=jax.ShapeDtypeStruct((FRONTS * layout[-1],), jnp.int32),
        scratch_shapes=[pltpu.SMEM((size,), jnp.int32)],
        name="block_table",
    )(index_maps, place)


TALL = 2
WIDE = 4


def extend_body(count, split, span, table, parent, *refs):
    arrays, refs = refs[: count * split], refs[count * split :]
    out, acc, lhs, rhs, sem, acc_sem = refs
    rows, cols = parent.shape
    nrb, ncb, strips, head, stride = table_layout(rows, cols)
    widths = [arrays[n * split].shape[1] for n in range(count)]

    def strip_copy(s, src, dst, way):
        here = pl.ds(s * (rows // strips), rows // strips)
        return pltpu.make_async_copy(src.at[here, :], dst.at[here, :], acc_sem.at[way, s])

    for s in range(strips):
        strip_copy(s, parent, acc, 0).start()

    def bring(f, first, total, dst):
        def one(i, _):
            code = table[f * stride + head + 1 + 2 * (first + i)]
            start = pl.multiple_of(code % span * BLK, BLK)
            at = pl.ds(pl.multiple_of(i * BLK, BLK), BLK)
            for a in range(split):

                @pl.when(code // span == a)
                def _():
                    for n in range(count):
                        where = pl.ds(sum(widths[:n]), widths[n])
                        pltpu.make_async_copy(
                            arrays[n * split + a].at[pl.ds(start, BLK), :],
                            dst.at[f, at, where],
                            sem.at[f],
                        ).start()

            return 0

        lax.fori_loop(0, total, one, 0)

    def drain(f, total):
        def one(_, carry):
            block = lhs.at[f, pl.ds(0, BLK), :]
            pltpu.make_async_copy(block, block, sem.at[f]).wait()
            return carry

        lax.fori_loop(0, total, one, 0)

    def present(f):
        return table[f * stride], table[f * stride + 1 + strips]

    for f in range(FRONTS):
        nc, nr = present(f)
        bring(f, 0, nr, lhs)
        bring(f, nrb, nc, rhs)

    def strip_front(f, s):
        nc, _ = present(f)
        first = table[f * stride + 1 + s]
        last = table[f * stride + 2 + s]

        def col_step(j, _):
            at = pl.multiple_of(j * WIDE * BLK, WIDE * BLK)
            right = rhs[f, pl.ds(at, WIDE * BLK), :]

            def row_step(i, _):
                top = first + i * TALL
                left = lhs[f, pl.ds(pl.multiple_of(top * BLK, BLK), TALL * BLK), :]
                prod = lax.dot_general(
                    left, right, (((1,), (1,)), ((), ())), preferred_element_type=F32
                )
                for b in range(WIDE):
                    c = table[f * stride + head + 2 * (nrb + jnp.minimum(j * WIDE + b, ncb - 1))]
                    c = jnp.where(j * WIDE + b < nc, c, 0)
                    for a in range(TALL):
                        r = table[f * stride + head + 2 * jnp.minimum(top + a, nrb - 1)]
                        real = (top + a < last) & (j * WIDE + b < nc)
                        r = jnp.where(real, r, nrb)
                        block = (
                            pl.ds(pl.multiple_of(r * BLK, BLK), BLK),
                            pl.ds(pl.multiple_of(c * BLK, BLK), BLK),
                        )
                        acc[block] -= prod[a * BLK : (a + 1) * BLK, b * BLK : (b + 1) * BLK]

                return 0

            lax.fori_loop(0, (last - first + TALL - 1) // TALL, row_step, 0)
            return 0

        lax.fori_loop(0, (nc + WIDE - 1) // WIDE, col_step, 0)

    for s in range(strips):
        strip_copy(s, parent, acc, 0).wait()

        def one_front(f, _):
            if s == 0:
                drain(f, table[f * stride] + table[f * stride + 1 + strips])
            strip_front(f, s)
            return 0

        lax.fori_loop(0, FRONTS, one_front, 0)
        strip_copy(s, acc, out, 1).start()
    for s in range(strips):
        strip_copy(s, acc, out, 1).wait()


def extend_add(parent, chunks, table, span, reuse):
    count, split = len(chunks), len(chunks[0])
    rows, cols = parent.shape
    nrb, ncb, strips = table_layout(rows, cols)[:3]
    depth = sum(chunk[0].shape[1] for chunk in chunks)
    return pl.pallas_call(
        functools.partial(extend_body, count, split, span),
        grid_spec=pltpu.PrefetchScalarGridSpec(
            num_scalar_prefetch=1,
            grid=(1,),
            in_specs=[HBM] * (1 + count * split),
            out_specs=HBM,
            scratch_shapes=[
                pltpu.VMEM((rows + BLK, cols), F32),
                pltpu.VMEM((FRONTS, (nrb + TALL) * BLK, depth), HALF),
                pltpu.VMEM((FRONTS, (ncb + WIDE) // WIDE * WIDE * BLK, depth), HALF),
                pltpu.SemaphoreType.DMA((FRONTS,)),
                pltpu.SemaphoreType.DMA((2, strips)),
            ],
        ),
        out_shape=jax.ShapeDtypeStruct((rows, cols), F32),
        input_output_aliases={1: 0} if reuse else {},
        compiler_params=pltpu.CompilerParams(vmem_limit_bytes=60 << 20),
        cost_estimate=pl.CostEstimate(
            flops=rows * cols * depth, bytes_accessed=64 << 20, transcendentals=0
        ),
        name="extend_add",
    )(table, parent, *[a for chunk in chunks for a in chunk])


def paired(size_grp, size_col, flip):
    route = []
    for g in range(size_grp):
        for c in range(size_col):
            to = flip(g, c)
            if to is not None:
                route.append((g * size_col + c, to[0] * size_col + to[1]))
    return route


def fronts_apart(diag_blocks, coupling, parent_front, index_maps):
    ng, nc = lax.axis_size("grp"), lax.axis_size("col")
    nz = nc // 2
    grp, col = lax.axis_index("grp"), lax.axis_index("col")
    width = diag_blocks.shape[1]
    blocks = coupling.shape[1] // width
    per = coupling.shape[0] // BLK
    nrows = parent_front.shape[0] * ng

    def send(block, flip):
        return lax.ppermute(block, ("grp", "col"), paired(ng, nc, flip))

    def along_z(rows, first, last):
        own = lax.slice_in_dim(rows, first * width, last * width, axis=0)
        pile = [own]
        for dz in range(1, nz):
            pile.append(send(own, lambda g, c: (g, c ^ 2 * dz) if c >= first else None))
        return pile

    def across_y(pile):
        near = jnp.concatenate(pile, axis=0)
        return near, send(near, lambda g, c: (g, c ^ 1))

    def one_way(g, c):
        return (g ^ 2, c) if g % 2 == 0 else (g, c ^ 1)

    def other_way(g, c):
        return (g, c ^ 1) if g % 2 == 0 else (g ^ 2, c)

    def other_core(g, c):
        return (g ^ 1, c)

    def advance(stage, held):
        if stage == 0:
            (half,) = held
            return [half] + [send(half, lambda g, c: (g, c ^ 2 * dz)) for dz in range(1, nz)]
        if stage == 1:
            own = jnp.concatenate(held, axis=0)
            return [own, send(own, one_way)]
        if stage == 2:
            return held + [send(a, other_way) for a in held]
        return held + [send(a, other_core) for a in held]

    cuts = [0, 1, 2, *range(4, blocks, 2), blocks]
    spans = list(zip(cuts, cuts[1:]))
    lead = 2
    z_slot = {0: -2, 1: -1, 2: 0}
    y_slot = {0: -1, 1: 0, 2: 1}
    for n in range(3, len(spans)):
        z_slot[n] = 0 if n == len(spans) - 1 else n - 2
        y_slot[n] = z_slot[n] + 1
    band_of = {k: n for n, (a, b) in enumerate(spans) for k in range(a, b)}
    place = jnp.stack([grp, col]).astype(jnp.int32)
    col_id = place[1:]
    span = nz * per
    table = None
    rows_left = diag_blocks
    u_all = x_all = None
    merged = parent_front
    piles, bands = {}, {}
    flying, done, stages = {}, {}, 4
    added = 0
    for slot in range(-lead, blocks + stages):
        for n in flying:
            if done[n] < stages:
                flying[n] = advance(done[n], flying[n])
                done[n] += 1
        for n in range(len(spans)):
            if y_slot[n] == slot:
                bands[n] = across_y(piles.pop(n))
            if z_slot[n] == slot:
                piles[n] = along_z(rows_left, *spans[n])
        if 0 <= slot < blocks:
            n = band_of[slot]
            u_all, x_all, half = factor_step(
                slot, *spans[n], bands[n], coupling, u_all, x_all, col_id
            )
            flying[slot], done[slot] = [half], 0
        if slot == stages:
            table = block_table(index_maps, place, per, span, nrows // BLK, parent_front.shape)
        if slot == blocks:
            ready = range(added, blocks - stages)
            merged = extend_add(merged, [flying[n] for n in ready], table, span, added > 0)
            added = ready.stop
        flying, piles, bands, u_all, x_all, merged, index_maps, table, rows_left = (
            lax.optimization_barrier(
                (flying, piles, bands, u_all, x_all, merged, index_maps, table, rows_left)
            )
        )
    chunks = [flying[n] for n in range(added, blocks)]
    merged = extend_add(merged, chunks, table, span, added > 0)
    mine = lax.dynamic_slice_in_dim(u_all, col * width, width, 0)
    return (merged, mine.T, x_all)


def on_device(diag_blocks, coupling, parent_front, index_maps):
    ng, nc = lax.axis_size("grp"), lax.axis_size("col")
    simple = (
        ng == FRONTS
        and nc % 2 == 0
        and nc & (nc - 1) == 0
        and diag_blocks.shape[1] == BLK
        and coupling.shape[0] % BLK == 0
    )
    body = fronts_apart if simple else general
    return body(diag_blocks, coupling, parent_front, index_maps)


def solution(mesh):
    in_specs = (P("grp", "col"), P(("grp", "col"), None), P("grp", "col"), P())
    out_specs = (P("grp", "col"), P("grp", "col"), P(("grp", "col"), None))
    return jax.shard_map(
        on_device, mesh=mesh, in_specs=in_specs, out_specs=out_specs, check_vma=False
    )
```

```python
import functools

import jax
import jax.numpy as jnp
from jax import lax
from jax.experimental import pallas as pl
from jax.experimental.pallas import tpu as pltpu
from jax.sharding import PartitionSpec as P

FRONTS = 4
BLK = 128
SBLK = 48
PBLK = 96
F32 = jnp.float32
HALF = jnp.bfloat16
EXACT = lax.Precision.HIGHEST
HBM = pl.BlockSpec(memory_space=pltpu.HBM)


def swapped(block, axis, stride):
    count = lax.axis_size(axis)
    route = []
    for low in range(count):
        high = low | 1 << stride
        if high != low and high < count:
            route += [(low, high), (high, low)]
    return lax.ppermute(block, axis, route)


def place_rows(slab_blocks, source_block, present_count, count):
    picked = slab_blocks[jnp.arange(FRONTS)[:, None], source_block]
    picked = jnp.where(present_count[:, :, None, None] > 0, picked, jnp.zeros_like(picked))
    return jnp.transpose(picked, (1, 2, 0, 3)).reshape(count * BLK, -1)


def general(diag_blocks, coupling, parent_front, index_maps):
    groups = lax.axis_size("grp") // FRONTS
    swap_depth = groups.bit_length() - 1
    grp_index = lax.axis_index("grp")
    col_index = lax.axis_index("col")
    gathered = lax.all_gather(diag_blocks, "col", axis=1, tiled=True)
    for bit_pos in range(swap_depth):
        partner = swapped(gathered, "grp", bit_pos)
        is_upper = grp_index // 2**bit_pos % 2 == 1
        lower_half = jnp.where(is_upper, partner, gathered)
        upper_half = jnp.where(is_upper, gathered, partner)
        gathered = jnp.concatenate([lower_half, upper_half], axis=0)
    factor = jnp.linalg.cholesky(gathered)
    rows_here = diag_blocks.shape[0]
    col_width = diag_blocks.shape[1]
    local_start = grp_index % groups * rows_here
    factor_tile = lax.dynamic_slice(
        factor, (local_start, col_index * col_width), (rows_here, col_width)
    )
    panel_rows = lax.linalg.triangular_solve(
        factor, coupling, left_side=False, lower=True, transpose_a=True
    )
    panel_half = panel_rows.astype(HALF)
    panel_tiles = lax.all_to_all(panel_half, "col", split_axis=1, concat_axis=0, tiled=True)
    panel_slab = lax.all_gather(panel_tiles, "grp", axis=0, tiled=True)
    slab_blocks = panel_slab.reshape(FRONTS, SBLK, BLK, -1)
    parent_ids = jnp.arange(PBLK, dtype=jnp.int32)
    matches = (index_maps[:, :, None] == parent_ids[None, None, :]).astype(jnp.int32)
    present_count = jnp.sum(matches, axis=1)
    source_block = jnp.sum(matches * jnp.arange(SBLK, dtype=jnp.int32)[None, :, None], axis=1)
    row_count = parent_front.shape[0]
    contract = (((1,), (1,)), ((), ()))
    every_part = place_rows(slab_blocks, source_block, present_count, PBLK)
    col_operand = lax.all_to_all(every_part, "col", split_axis=0, concat_axis=1, tiled=True)
    row_part = lax.dynamic_slice_in_dim(every_part, grp_index * row_count, row_count, 0)
    update = lax.dot_general(
        lax.all_gather(row_part, "col", axis=1, tiled=True),
        col_operand,
        contract,
        preferred_element_type=F32,
    )
    return (parent_front - update, factor_tile, panel_rows)


def dot(a, b, ca, cb):
    return lax.dot_general(
        a, b, (((ca,), (cb,)), ((), ())), precision=EXACT, preferred_element_type=F32
    )


def eliminate(s_val, u_ref, inv_ref, width):
    rows = 8
    shape = (width, width)
    eye = lax.broadcasted_iota(jnp.int32, shape, 0) == lax.broadcasted_iota(jnp.int32, shape, 1)
    sub = lax.broadcasted_iota(jnp.int32, (rows, width), 0)

    def group(g, carry):
        s, e = carry
        top_s, top_e = s[:rows], e[:rows]
        cols = [jnp.broadcast_to(top_s[:, i : i + 1], (rows, width)) for i in range(rows)]
        u_s = jnp.zeros_like(top_s)
        u_e = jnp.zeros_like(top_e)
        for i in range(rows):
            me = sub == i
            root = lax.rsqrt(cols[i][i : i + 1, :])
            inv = root * root
            u_s = jnp.where(me, top_s * root, u_s)
            u_e = jnp.where(me, top_e * root, u_e)
            for j in range(i + 1, rows):
                w = cols[j][i : i + 1, :] * inv
                cols[j] = jnp.where(me, w, cols[j] - cols[i] * w)
            w_s = top_s[i : i + 1, :] * inv
            w_e = top_e[i : i + 1, :] * inv
            top_s = jnp.where(me, w_s, top_s - cols[i] * w_s)
            top_e = jnp.where(me, w_e, top_e - cols[i] * w_e)
        rest_s, rest_e = s[rows:], e[rows:]
        heads = [rest_s[:, i : i + 1] for i in range(rows)]
        for i in range(rows):
            rest_s = rest_s - heads[i] * top_s[i : i + 1, :]
            rest_e = rest_e - heads[i] * top_e[i : i + 1, :]
        at = pl.multiple_of(g * rows, rows)
        u_ref[pl.ds(at, rows), :] = pltpu.roll(u_s, at, 1)
        inv_ref[pl.ds(at, rows), :] = u_e
        s = jnp.concatenate([rest_s, s[:rows]], axis=0)
        e = jnp.concatenate([rest_e, e[:rows]], axis=0)
        return pltpu.roll(s, width - rows, 1), e

    lax.fori_loop(0, width // rows, group, (s_val, eye.astype(F32)))


def factor_body(k, width, cols, col_ref, *refs):
    pieces, c_ref, refs = refs[:cols], refs[cols], refs[cols + 1 :]
    if k:
        u_in, x_in, refs = refs[0], refs[1], refs[2:]
    u_out, x_out, half_ref, u_v, x_v, s_v, t_v, uk_v, inv_v, sem = refs
    n = s_v.shape[1]
    base = k * width
    rest = n - base - width
    here = pl.ds(base, width)
    if k:
        before = pl.ds(0, base)
        load_u = pltpu.make_async_copy(u_in.at[before, :], u_v.at[before, :], sem.at[0])
        load_x = pltpu.make_async_copy(x_in.at[:, before], x_v.at[:, before], sem.at[1])
        load_u.start()
        load_x.start()
    for rel in range(cols):
        at = pl.multiple_of((col_ref[0] ^ rel) * width, width)
        s_v[:, pl.ds(at, width)] = pieces[rel][...]
    if k:
        load_u.wait()

        def prev(j, _):
            at = pl.multiple_of(j * width, width)
            uj = u_v[pl.ds(at, width), pl.ds(base, n - base)]
            s_v[:, pl.ds(base, n - base)] -= dot(uj[:, :width], uj, 0, 0)
            return 0

        lax.fori_loop(0, k, prev, 0)
    eliminate(s_v[:, here], uk_v, inv_v, width)
    inv = inv_v[...]
    r = lax.broadcasted_iota(jnp.int32, (width, width), 0)
    c = lax.broadcasted_iota(jnp.int32, (width, width), 1)
    if base:
        u_v[here, pl.ds(0, base)] = jnp.zeros((width, base), F32)
    u_v[here, here] = jnp.where(c >= r, uk_v[...], 0.0)
    if rest:
        right = pl.ds(base + width, rest)
        u_v[here, right] = dot(inv, s_v[:, right], 1, 0)
    save_u = pltpu.make_async_copy(u_v.at[here, :], u_out.at[here, :], sem.at[2])
    save_u.start()
    t_v[...] = c_ref[...]
    if k:
        load_x.wait()

        def prevx(j, _):
            at = pl.multiple_of(j * width, width)
            t_v[...] -= dot(x_v[:, pl.ds(at, width)], u_v[pl.ds(at, width), here], 1, 0)
            return 0

        lax.fori_loop(0, k, prevx, 0)
    x_v[:, here] = dot(t_v[...], inv, 1, 1)
    half_ref[...] = x_v[:, here].astype(HALF)
    save_x = pltpu.make_async_copy(x_v.at[:, here], x_out.at[:, here], sem.at[3])
    save_x.start()
    save_u.wait()
    save_x.wait()


def factor_step(k, first, last, band, coupling, u_all, x_all, col_id):
    m, n = coupling.shape
    width = band[0].shape[1]
    cols = n // width
    args, specs = [], []
    for rel in range(cols):
        at = rel // 2 * (last - first) + k - first
        args.append(band[rel % 2])
        specs.append(pl.BlockSpec((width, width), lambda i, s, at=at: (at, 0)))
    args.append(coupling)
    specs += [pl.BlockSpec((m, width), lambda i, s: (0, k))]
    alias = {}
    if k:
        alias = {len(args) + 1: 0, len(args) + 2: 1}
        args += [u_all, x_all]
        specs += [HBM, HBM]
    square = pltpu.VMEM((width, width), F32)
    return pl.pallas_call(
        functools.partial(factor_body, k, width, cols),
        grid_spec=pltpu.PrefetchScalarGridSpec(
            num_scalar_prefetch=1,
            grid=(1,),
            in_specs=specs,
            out_specs=(HBM, HBM, pl.BlockSpec((m, width), lambda i, s: (0, 0))),
            scratch_shapes=[
                pltpu.VMEM((n, n), F32),
                pltpu.VMEM((m, n), F32),
                pltpu.VMEM((width, n), F32),
                pltpu.VMEM((m, width), F32),
                square,
                square,
                pltpu.SemaphoreType.DMA((4,)),
            ],
        ),
        out_shape=(
            jax.ShapeDtypeStruct((n, n), F32),
            jax.ShapeDtypeStruct((m, n), F32),
            jax.ShapeDtypeStruct((m, width), HALF),
        ),
        input_output_aliases=alias,
        compiler_params=pltpu.CompilerParams(vmem_limit_bytes=60 << 20),
        cost_estimate=pl.CostEstimate(
            flops=10**9, bytes_accessed=48 << 20, transcendentals=0
        ),
        name=f"factor{k}",
    )(col_id, *args)


def table_layout(rows, cols):
    nrb, ncb = rows // BLK, cols // BLK
    strips = next(n for n in (3, 2, 1) if nrb % n == 0)
    head = strips + 2
    return nrb, ncb, strips, head, head + 2 * (nrb + ncb)


def table_body(per, span, layout, source, place, table):
    nrb, ncb, strips, head, stride = layout
    grp, col = place[0], place[1]
    x_at, core_at = grp // 2, grp % 2

    def front(f, _):
        base = f * stride

        def entry(where, p, i):
            dc = (f % 2) ^ core_at
            dx = (f // 2) ^ x_at
            dcol = (i // per) ^ col
            dy, dz = dcol % 2, dcol // 2
            near = jnp.where(f % 2 == 0, dx + 2 * dy, dy + 2 * dx)
            table[where] = p
            table[where + 1] = (4 * dc + near) * span + (dz * per + i % per)

        def row(p, n):
            i = source[f, grp * nrb + p]

            @pl.when(p % (nrb // strips) == 0)
            def _():
                table[base + 1 + p // (nrb // strips)] = n

            @pl.when(i >= 0)
            def _():
                entry(base + head + 2 * n, p, i)

            return n + (i >= 0).astype(jnp.int32)

        def column(p, n):
            i = source[f, col * ncb + p]

            @pl.when(i >= 0)
            def _():
                entry(base + head + 2 * (nrb + n), p, i)

            return n + (i >= 0).astype(jnp.int32)

        table[base + 1 + strips] = lax.fori_loop(0, nrb, row, jnp.int32(0))
        table[base] = lax.fori_loop(0, ncb, column, jnp.int32(0))
        return 0

    lax.fori_loop(0, FRONTS, front, 0)


def block_table(index_maps, place, per, span, size, shape):
    layout = table_layout(*shape)
    smem = pl.BlockSpec(memory_space=pltpu.SMEM)
    parents = jnp.arange(size, dtype=jnp.int32)[None, None, :]
    order = jnp.arange(1, index_maps.shape[1] + 1, dtype=jnp.int32)[None, :, None]
    source = jnp.sum(jnp.where(index_maps[:, :, None] == parents, order, 0), axis=1) - 1
    return pl.pallas_call(
        functools.partial(table_body, per, span, layout),
        in_specs=[smem, smem],
        out_specs=smem,
        out_shape=jax.ShapeDtypeStruct((FRONTS * layout[-1],), jnp.int32),
        name="block_table",
    )(source, place)


TALL = 2
WIDE = 4


def extend_body(count, split, span, tasks, aliased, table, parent, *refs):
    arrays, refs = refs[: count * split], refs[count * split :]
    out, acc, lhs, rhs, sem, acc_sem = refs[1:] if aliased else refs
    rows, cols = parent.shape
    nrb, ncb, strips, head, stride = table_layout(rows, cols)
    widths = [arrays[n * split].shape[1] for n in range(count)]

    def strip_copy(s, src, dst, way):
        here = pl.ds(s * (rows // strips), rows // strips)
        return pltpu.make_async_copy(src.at[here, :], dst.at[here, :], acc_sem.at[way, s])

    for s, _ in tasks:
        strip_copy(s, parent, acc, 0).start()

    def bring(f, base, first, last, dst):
        def one(i, _):
            code = table[f * stride + head + 1 + 2 * (base + i)]
            start = pl.multiple_of(code % span * BLK, BLK)
            at = pl.ds(pl.multiple_of(i * BLK, BLK), BLK)
            for a in range(split):

                @pl.when(code // span == a)
                def _():
                    for n in range(count):
                        where = pl.ds(sum(widths[:n]), widths[n])
                        pltpu.make_async_copy(
                            arrays[n * split + a].at[pl.ds(start, BLK), :],
                            dst.at[f, at, where],
                            sem.at[f],
                        ).start()

            return 0

        lax.fori_loop(first, last, one, 0)

    def drain(f, total):
        def one(_, carry):
            block = lhs.at[f, pl.ds(0, BLK), :]
            pltpu.make_async_copy(block, block, sem.at[f]).wait()
            return carry

        lax.fori_loop(0, total, one, 0)

    def present(f):
        first = table[f * stride + 1 + tasks[0][0]]
        last = table[f * stride + 2 + tasks[-1][0]]
        return table[f * stride], first, last

    for f in range(FRONTS):
        nc, first, last = present(f)
        bring(f, 0, first, last, lhs)
        bring(f, nrb, 0, nc, rhs)

    def strip_front(f, s, skip):
        nc = table[f * stride]
        first = table[f * stride + 1 + s]
        last = table[f * stride + 2 + s]
        deep = pl.ds(sum(widths[:skip]), sum(widths[skip:]))

        def col_step(j, _):
            at = pl.multiple_of(j * WIDE * BLK, WIDE * BLK)
            right = rhs[f, pl.ds(at, WIDE * BLK), deep]

            def row_step(i, _):
                top = first + i * TALL
                left = lhs[f, pl.ds(pl.multiple_of(top * BLK, BLK), TALL * BLK), deep]
                prod = lax.dot_general(
                    left, right, (((1,), (1,)), ((), ())), preferred_element_type=F32
                )
                for b in range(WIDE):
                    c = table[f * stride + head + 2 * (nrb + jnp.minimum(j * WIDE + b, ncb - 1))]
                    c = jnp.where(j * WIDE + b < nc, c, 0)
                    for a in range(TALL):
                        r = table[f * stride + head + 2 * jnp.minimum(top + a, nrb - 1)]
                        real = (top + a < last) & (j * WIDE + b < nc)
                        r = jnp.where(real, r, nrb)
                        block = (
                            pl.ds(pl.multiple_of(r * BLK, BLK), BLK),
                            pl.ds(pl.multiple_of(c * BLK, BLK), BLK),
                        )
                        acc[block] -= prod[a * BLK : (a + 1) * BLK, b * BLK : (b + 1) * BLK]

                return 0

            lax.fori_loop(0, (last - first + TALL - 1) // TALL, row_step, 0)
            return 0

        lax.fori_loop(0, (nc + WIDE - 1) // WIDE, col_step, 0)

    for s, skip in tasks:
        strip_copy(s, parent, acc, 0).wait()

        def one_front(f, _):
            if s == tasks[0][0]:
                nc, first, last = present(f)
                drain(f, nc + last - first)
            strip_front(f, s, skip)
            return 0

        lax.fori_loop(0, FRONTS, one_front, 0)
        strip_copy(s, acc, out, 1).start()
    for s, _ in tasks:
        strip_copy(s, acc, out, 1).wait()


def extend_add(parent, target, chunks, table, span, tasks):
    count, split = len(chunks), len(chunks[0])
    rows, cols = parent.shape
    nrb, ncb, strips = table_layout(rows, cols)[:3]
    depth = sum(chunk[0].shape[1] for chunk in chunks)
    args = [table, parent, *[a for chunk in chunks for a in chunk]]
    apart = target is not None and target is not parent
    alias = {} if target is None else {1: 0}
    if apart:
        alias = {len(args): 0}
        args.append(target)
    return pl.pallas_call(
        functools.partial(extend_body, count, split, span, tasks, apart),
        grid_spec=pltpu.PrefetchScalarGridSpec(
            num_scalar_prefetch=1,
            grid=(1,),
            in_specs=[HBM] * (len(args) - 1),
            out_specs=HBM,
            scratch_shapes=[
                pltpu.VMEM((rows + BLK, cols), F32),
                pltpu.VMEM((FRONTS, (nrb + TALL) * BLK, depth), HALF),
                pltpu.VMEM((FRONTS, (ncb + WIDE) // WIDE * WIDE * BLK, depth), HALF),
                pltpu.SemaphoreType.DMA((FRONTS,)),
                pltpu.SemaphoreType.DMA((2, strips)),
            ],
        ),
        out_shape=jax.ShapeDtypeStruct((rows, cols), F32),
        input_output_aliases=alias,
        compiler_params=pltpu.CompilerParams(vmem_limit_bytes=60 << 20),
        cost_estimate=pl.CostEstimate(
            flops=rows * cols * depth * len(tasks) // strips,
            bytes_accessed=len(tasks) * (16 << 20),
            transcendentals=0,
        ),
        name="extend_add",
    )(*args)


def paired(size_grp, size_col, flip):
    route = []
    for g in range(size_grp):
        for c in range(size_col):
            to = flip(g, c)
            if to is not None:
                route.append((g * size_col + c, to[0] * size_col + to[1]))
    return route


def fronts_apart(diag_blocks, coupling, parent_front, index_maps):
    ng, nc = lax.axis_size("grp"), lax.axis_size("col")
    nz = nc // 2
    grp, col = lax.axis_index("grp"), lax.axis_index("col")
    width = diag_blocks.shape[1]
    blocks = coupling.shape[1] // width
    per = coupling.shape[0] // BLK
    nrows = parent_front.shape[0] * ng

    def send(block, flip):
        return lax.ppermute(block, ("grp", "col"), paired(ng, nc, flip))

    def along_z(rows, first, last):
        own = lax.slice_in_dim(rows, first * width, last * width, axis=0)
        pile = [own]
        for dz in range(1, nz):
            pile.append(send(own, lambda g, c: (g, c ^ 2 * dz) if c >= first else None))
        return pile

    def across_y(pile):
        near = jnp.concatenate(pile, axis=0)
        return near, send(near, lambda g, c: (g, c ^ 1))

    def one_way(g, c):
        return (g ^ 2, c) if g % 2 == 0 else (g, c ^ 1)

    def other_way(g, c):
        return (g, c ^ 1) if g % 2 == 0 else (g ^ 2, c)

    def other_core(g, c):
        return (g ^ 1, c)

    def advance(stage, held):
        if stage == 0:
            (half,) = held
            return [half] + [send(half, lambda g, c: (g, c ^ 2 * dz)) for dz in range(1, nz)]
        if stage == 1:
            own = jnp.concatenate(held, axis=0)
            return [own, send(own, one_way)]
        if stage == 2:
            return held + [send(a, other_way) for a in held]
        return held + [send(a, other_core) for a in held]

    cuts = [0, 1, 2, *range(4, blocks, 2), blocks]
    spans = list(zip(cuts, cuts[1:]))
    lead = 2
    z_slot = {0: -2, 1: -1, 2: 0}
    y_slot = {0: -1, 1: 0, 2: 1}
    for n in range(3, len(spans)):
        z_slot[n] = 0 if n == len(spans) - 1 else n - 2
        y_slot[n] = z_slot[n] + 1
    band_of = {k: n for n, (a, b) in enumerate(spans) for k in range(a, b)}
    place = jnp.stack([grp, col]).astype(jnp.int32)
    col_id = place[1:]
    span = nz * per
    table = None
    rows_left = diag_blocks
    u_all = x_all = None
    merged = None
    piles, bands = {}, {}
    flying, done, stages = {}, {}, 4
    added = []
    strips = table_layout(*parent_front.shape)[2]
    for slot in range(-lead, blocks + stages):
        for n in flying:
            if done[n] < stages:
                flying[n] = advance(done[n], flying[n])
                done[n] += 1
        for n in range(len(spans)):
            if y_slot[n] == slot:
                bands[n] = across_y(piles.pop(n))
            if z_slot[n] == slot:
                piles[n] = along_z(rows_left, *spans[n])
        if 0 <= slot < blocks:
            n = band_of[slot]
            u_all, x_all, half = factor_step(
                slot, *spans[n], bands[n], coupling, u_all, x_all, col_id
            )
            flying[slot], done[slot] = [half], 0
        if slot == stages:
            table = block_table(index_maps, place, per, span, nrows // BLK, parent_front.shape)
        strip = slot - blocks
        if 0 <= strip < strips and strip < stages - 1:
            ready = [flying[n] for n in range(slot - stages)]
            merged = extend_add(parent_front, merged, ready, table, span, ((strip, 0),))
            added.append(slot - stages)
        flying, piles, bands, u_all, x_all, merged, index_maps, table, rows_left = (
            lax.optimization_barrier(
                (flying, piles, bands, u_all, x_all, merged, index_maps, table, rows_left)
            )
        )
    chunks = [flying[n] for n in range(added[0], blocks)]
    tasks = tuple((n, at - added[0]) for n, at in enumerate(added))
    merged = extend_add(merged, merged, chunks, table, span, tasks)
    mine = lax.dynamic_slice_in_dim(u_all, col * width, width, 0)
    return (merged, mine.T, x_all)


def on_device(diag_blocks, coupling, parent_front, index_maps):
    ng, nc = lax.axis_size("grp"), lax.axis_size("col")
    simple = (
        ng == FRONTS
        and nc % 2 == 0
        and nc & (nc - 1) == 0
        and diag_blocks.shape[1] == BLK
        and coupling.shape[0] % BLK == 0
    )
    body = fronts_apart if simple else general
    return body(diag_blocks, coupling, parent_front, index_maps)


def solution(mesh):
    in_specs = (P("grp", "col"), P(("grp", "col"), None), P("grp", "col"), P())
    out_specs = (P("grp", "col"), P("grp", "col"), P(("grp", "col"), None))
    return jax.shard_map(
        on_device, mesh=mesh, in_specs=in_specs, out_specs=out_specs, check_vma=False
    )
```

```python
import functools

import jax
import jax.numpy as jnp
from jax import lax
from jax.experimental import pallas as pl
from jax.experimental.pallas import tpu as pltpu
from jax.sharding import PartitionSpec as P

FRONTS = 4
BLK = 128
SBLK = 48
PBLK = 96
F32 = jnp.float32
HALF = jnp.bfloat16
EXACT = lax.Precision.HIGHEST
HBM = pl.BlockSpec(memory_space=pltpu.HBM)


def swapped(block, axis, stride):
    count = lax.axis_size(axis)
    route = []
    for low in range(count):
        high = low | 1 << stride
        if high != low and high < count:
            route += [(low, high), (high, low)]
    return lax.ppermute(block, axis, route)


def place_rows(slab_blocks, source_block, present_count, count):
    picked = slab_blocks[jnp.arange(FRONTS)[:, None], source_block]
    picked = jnp.where(present_count[:, :, None, None] > 0, picked, jnp.zeros_like(picked))
    return jnp.transpose(picked, (1, 2, 0, 3)).reshape(count * BLK, -1)


def general(diag_blocks, coupling, parent_front, index_maps):
    groups = lax.axis_size("grp") // FRONTS
    swap_depth = groups.bit_length() - 1
    grp_index = lax.axis_index("grp")
    col_index = lax.axis_index("col")
    gathered = lax.all_gather(diag_blocks, "col", axis=1, tiled=True)
    for bit_pos in range(swap_depth):
        partner = swapped(gathered, "grp", bit_pos)
        is_upper = grp_index // 2**bit_pos % 2 == 1
        lower_half = jnp.where(is_upper, partner, gathered)
        upper_half = jnp.where(is_upper, gathered, partner)
        gathered = jnp.concatenate([lower_half, upper_half], axis=0)
    factor = jnp.linalg.cholesky(gathered)
    rows_here = diag_blocks.shape[0]
    col_width = diag_blocks.shape[1]
    local_start = grp_index % groups * rows_here
    factor_tile = lax.dynamic_slice(
        factor, (local_start, col_index * col_width), (rows_here, col_width)
    )
    panel_rows = lax.linalg.triangular_solve(
        factor, coupling, left_side=False, lower=True, transpose_a=True
    )
    panel_half = panel_rows.astype(HALF)
    panel_tiles = lax.all_to_all(panel_half, "col", split_axis=1, concat_axis=0, tiled=True)
    panel_slab = lax.all_gather(panel_tiles, "grp", axis=0, tiled=True)
    slab_blocks = panel_slab.reshape(FRONTS, SBLK, BLK, -1)
    parent_ids = jnp.arange(PBLK, dtype=jnp.int32)
    matches = (index_maps[:, :, None] == parent_ids[None, None, :]).astype(jnp.int32)
    present_count = jnp.sum(matches, axis=1)
    source_block = jnp.sum(matches * jnp.arange(SBLK, dtype=jnp.int32)[None, :, None], axis=1)
    row_count = parent_front.shape[0]
    contract = (((1,), (1,)), ((), ()))
    every_part = place_rows(slab_blocks, source_block, present_count, PBLK)
    col_operand = lax.all_to_all(every_part, "col", split_axis=0, concat_axis=1, tiled=True)
    row_part = lax.dynamic_slice_in_dim(every_part, grp_index * row_count, row_count, 0)
    update = lax.dot_general(
        lax.all_gather(row_part, "col", axis=1, tiled=True),
        col_operand,
        contract,
        preferred_element_type=F32,
    )
    return (parent_front - update, factor_tile, panel_rows)


def dot(a, b, ca, cb):
    return lax.dot_general(
        a, b, (((ca,), (cb,)), ((), ())), precision=EXACT, preferred_element_type=F32
    )


def eliminate(s_val, u_ref, inv_ref, width):
    rows = 8
    shape = (width, width)
    eye = lax.broadcasted_iota(jnp.int32, shape, 0) == lax.broadcasted_iota(jnp.int32, shape, 1)
    sub = lax.broadcasted_iota(jnp.int32, (rows, width), 0)

    def group(g, carry):
        s, e = carry
        top_s, top_e = s[:rows], e[:rows]
        cols = [jnp.broadcast_to(top_s[:, i : i + 1], (rows, width)) for i in range(rows)]
        u_s = jnp.zeros_like(top_s)
        u_e = jnp.zeros_like(top_e)
        for i in range(rows):
            me = sub == i
            root = lax.rsqrt(cols[i][i : i + 1, :])
            inv = root * root
            u_s = jnp.where(me, top_s * root, u_s)
            u_e = jnp.where(me, top_e * root, u_e)
            for j in range(i + 1, rows):
                w = cols[j][i : i + 1, :] * inv
                cols[j] = jnp.where(me, w, cols[j] - cols[i] * w)
            w_s = top_s[i : i + 1, :] * inv
            w_e = top_e[i : i + 1, :] * inv
            top_s = jnp.where(me, w_s, top_s - cols[i] * w_s)
            top_e = jnp.where(me, w_e, top_e - cols[i] * w_e)
        rest_s, rest_e = s[rows:], e[rows:]
        heads = [rest_s[:, i : i + 1] for i in range(rows)]
        for i in range(rows):
            rest_s = rest_s - heads[i] * top_s[i : i + 1, :]
            rest_e = rest_e - heads[i] * top_e[i : i + 1, :]
        at = pl.multiple_of(g * rows, rows)
        u_ref[pl.ds(at, rows), :] = pltpu.roll(u_s, at, 1)
        inv_ref[pl.ds(at, rows), :] = u_e
        s = jnp.concatenate([rest_s, s[:rows]], axis=0)
        e = jnp.concatenate([rest_e, e[:rows]], axis=0)
        return pltpu.roll(s, width - rows, 1), e

    lax.fori_loop(0, width // rows, group, (s_val, eye.astype(F32)))


def factor_body(k, width, cols, col_ref, *refs):
    pieces, c_ref, refs = refs[:cols], refs[cols], refs[cols + 1 :]
    if k:
        u_in, x_in, refs = refs[0], refs[1], refs[2:]
    u_out, x_out, half_ref, u_v, x_v, s_v, t_v, uk_v, inv_v, sem = refs
    n = s_v.shape[1]
    base = k * width
    rest = n - base - width
    here = pl.ds(base, width)
    if k:
        before = pl.ds(0, base)
        load_u = pltpu.make_async_copy(u_in.at[before, :], u_v.at[before, :], sem.at[0])
        load_x = pltpu.make_async_copy(x_in.at[:, before], x_v.at[:, before], sem.at[1])
        load_u.start()
        load_x.start()
    for rel in range(cols):
        at = pl.multiple_of((col_ref[0] ^ rel) * width, width)
        s_v[:, pl.ds(at, width)] = pieces[rel][...]
    if k:
        load_u.wait()

        def prev(j, _):
            at = pl.multiple_of(j * width, width)
            uj = u_v[pl.ds(at, width), pl.ds(base, n - base)]
            s_v[:, pl.ds(base, n - base)] -= dot(uj[:, :width], uj, 0, 0)
            return 0

        lax.fori_loop(0, k, prev, 0)
    eliminate(s_v[:, here], uk_v, inv_v, width)
    inv = inv_v[...]
    r = lax.broadcasted_iota(jnp.int32, (width, width), 0)
    c = lax.broadcasted_iota(jnp.int32, (width, width), 1)
    if base:
        u_v[here, pl.ds(0, base)] = jnp.zeros((width, base), F32)
    u_v[here, here] = jnp.where(c >= r, uk_v[...], 0.0)
    if rest:
        right = pl.ds(base + width, rest)
        u_v[here, right] = dot(inv, s_v[:, right], 1, 0)
    save_u = pltpu.make_async_copy(u_v.at[here, :], u_out.at[here, :], sem.at[2])
    save_u.start()
    t_v[...] = c_ref[...]
    if k:
        load_x.wait()

        def prevx(j, _):
            at = pl.multiple_of(j * width, width)
            t_v[...] -= dot(x_v[:, pl.ds(at, width)], u_v[pl.ds(at, width), here], 1, 0)
            return 0

        lax.fori_loop(0, k, prevx, 0)
    x_v[:, here] = dot(t_v[...], inv, 1, 1)
    half_ref[...] = x_v[:, here].astype(HALF)
    save_x = pltpu.make_async_copy(x_v.at[:, here], x_out.at[:, here], sem.at[3])
    save_x.start()
    save_u.wait()
    save_x.wait()


def factor_step(k, first, last, band, coupling, u_all, x_all, col_id):
    m, n = coupling.shape
    width = band[0].shape[1]
    cols = n // width
    args, specs = [], []
    for rel in range(cols):
        at = rel // 2 * (last - first) + k - first
        args.append(band[rel % 2])
        specs.append(pl.BlockSpec((width, width), lambda i, s, at=at: (at, 0)))
    args.append(coupling)
    specs += [pl.BlockSpec((m, width), lambda i, s: (0, k))]
    alias = {}
    if k:
        alias = {len(args) + 1: 0, len(args) + 2: 1}
        args += [u_all, x_all]
        specs += [HBM, HBM]
    square = pltpu.VMEM((width, width), F32)
    return pl.pallas_call(
        functools.partial(factor_body, k, width, cols),
        grid_spec=pltpu.PrefetchScalarGridSpec(
            num_scalar_prefetch=1,
            grid=(1,),
            in_specs=specs,
            out_specs=(HBM, HBM, pl.BlockSpec((m, width), lambda i, s: (0, 0))),
            scratch_shapes=[
                pltpu.VMEM((n, n), F32),
                pltpu.VMEM((m, n), F32),
                pltpu.VMEM((width, n), F32),
                pltpu.VMEM((m, width), F32),
                square,
                square,
                pltpu.SemaphoreType.DMA((4,)),
            ],
        ),
        out_shape=(
            jax.ShapeDtypeStruct((n, n), F32),
            jax.ShapeDtypeStruct((m, n), F32),
            jax.ShapeDtypeStruct((m, width), HALF),
        ),
        input_output_aliases=alias,
        compiler_params=pltpu.CompilerParams(vmem_limit_bytes=60 << 20),
        cost_estimate=pl.CostEstimate(
            flops=10**9, bytes_accessed=48 << 20, transcendentals=0
        ),
        name=f"factor{k}",
    )(col_id, *args)


def table_layout(rows, cols):
    nrb, ncb = rows // BLK, cols // BLK
    strips = next(n for n in (3, 2, 1) if nrb % n == 0)
    head = strips + 2
    return nrb, ncb, strips, head, head + 2 * (nrb + ncb)


def table_body(per, span, layout, source, place, table):
    nrb, ncb, strips, head, stride = layout
    grp, col = place[0], place[1]
    x_at, core_at = grp // 2, grp % 2

    def front(f, _):
        base = f * stride

        def entry(where, p, i):
            dc = (f % 2) ^ core_at
            dx = (f // 2) ^ x_at
            dcol = (i // per) ^ col
            dy, dz = dcol % 2, dcol // 2
            near = jnp.where(f % 2 == 0, dx + 2 * dy, dy + 2 * dx)
            table[where] = p
            table[where + 1] = (4 * dc + near) * span + (dz * per + i % per)

        def row(p, n):
            i = source[f, grp * nrb + p]

            @pl.when(p % (nrb // strips) == 0)
            def _():
                table[base + 1 + p // (nrb // strips)] = n

            @pl.when(i >= 0)
            def _():
                entry(base + head + 2 * n, p, i)

            return n + (i >= 0).astype(jnp.int32)

        def column(p, n):
            i = source[f, col * ncb + p]

            @pl.when(i >= 0)
            def _():
                entry(base + head + 2 * (nrb + n), p, i)

            return n + (i >= 0).astype(jnp.int32)

        table[base + 1 + strips] = lax.fori_loop(0, nrb, row, jnp.int32(0))
        table[base] = lax.fori_loop(0, ncb, column, jnp.int32(0))
        return 0

    lax.fori_loop(0, FRONTS, front, 0)


def block_table(index_maps, place, per, span, size, shape):
    layout = table_layout(*shape)
    smem = pl.BlockSpec(memory_space=pltpu.SMEM)
    parents = jnp.arange(size, dtype=jnp.int32)[None, None, :]
    order = jnp.arange(1, index_maps.shape[1] + 1, dtype=jnp.int32)[None, :, None]
    source = jnp.sum(jnp.where(index_maps[:, :, None] == parents, order, 0), axis=1) - 1
    return pl.pallas_call(
        functools.partial(table_body, per, span, layout),
        in_specs=[smem, smem],
        out_specs=smem,
        out_shape=jax.ShapeDtypeStruct((FRONTS * layout[-1],), jnp.int32),
        name="block_table",
    )(source, place)


TALL = 2
WIDE = 4


def extend_body(count, split, span, tasks, aliased, table, parent, *refs):
    arrays, refs = refs[: count * split], refs[count * split :]
    out, acc, lhs, rhs, sem, acc_sem = refs[1:] if aliased else refs
    rows, cols = parent.shape
    nrb, ncb, strips, head, stride = table_layout(rows, cols)
    widths = [arrays[n * split].shape[1] for n in range(count)]

    def strip_copy(s, src, dst, way):
        here = pl.ds(s * (rows // strips), rows // strips)
        return pltpu.make_async_copy(src.at[here, :], dst.at[here, :], acc_sem.at[way, s])

    for s, _ in tasks:
        strip_copy(s, parent, acc, 0).start()

    def bring(f, base, first, last, dst):
        def one(i, _):
            code = table[f * stride + head + 1 + 2 * (base + i)]
            start = pl.multiple_of(code % span * BLK, BLK)
            at = pl.ds(pl.multiple_of(i * BLK, BLK), BLK)
            for a in range(split):

                @pl.when(code // span == a)
                def _():
                    for n in range(count):
                        where = pl.ds(sum(widths[:n]), widths[n])
                        pltpu.make_async_copy(
                            arrays[n * split + a].at[pl.ds(start, BLK), :],
                            dst.at[f, at, where],
                            sem.at[f],
                        ).start()

            return 0

        lax.fori_loop(first, last, one, 0)

    def drain(f, total):
        def one(_, carry):
            block = lhs.at[f, pl.ds(0, BLK), :]
            pltpu.make_async_copy(block, block, sem.at[f]).wait()
            return carry

        lax.fori_loop(0, total, one, 0)

    def present(f):
        first = table[f * stride + 1 + tasks[0][0]]
        last = table[f * stride + 2 + tasks[-1][0]]
        return table[f * stride], first, last

    for f in range(FRONTS):
        nc, first, last = present(f)
        bring(f, 0, first, last, lhs)
        bring(f, nrb, 0, nc, rhs)

    def strip_front(f, s, skip):
        nc = table[f * stride]
        first = table[f * stride + 1 + s]
        last = table[f * stride + 2 + s]
        deep = pl.ds(sum(widths[:skip]), sum(widths[skip:]))

        def col_step(j, _):
            at = pl.multiple_of(j * WIDE * BLK, WIDE * BLK)
            right = rhs[f, pl.ds(at, WIDE * BLK), deep]

            def row_step(i, _):
                top = first + i * TALL
                left = lhs[f, pl.ds(pl.multiple_of(top * BLK, BLK), TALL * BLK), deep]
                prod = lax.dot_general(
                    left, right, (((1,), (1,)), ((), ())), preferred_element_type=F32
                )
                for b in range(WIDE):
                    c = table[f * stride + head + 2 * (nrb + jnp.minimum(j * WIDE + b, ncb - 1))]
                    c = jnp.where(j * WIDE + b < nc, c, 0)
                    for a in range(TALL):
                        r = table[f * stride + head + 2 * jnp.minimum(top + a, nrb - 1)]
                        real = (top + a < last) & (j * WIDE + b < nc)
                        r = jnp.where(real, r, nrb)
                        block = (
                            pl.ds(pl.multiple_of(r * BLK, BLK), BLK),
                            pl.ds(pl.multiple_of(c * BLK, BLK), BLK),
                        )
                        acc[block] -= prod[a * BLK : (a + 1) * BLK, b * BLK : (b + 1) * BLK]

                return 0

            lax.fori_loop(0, (last - first + TALL - 1) // TALL, row_step, 0)
            return 0

        lax.fori_loop(0, (nc + WIDE - 1) // WIDE, col_step, 0)

    for s, skip in tasks:
        strip_copy(s, parent, acc, 0).wait()

        def one_front(f, _):
            if s == tasks[0][0]:
                nc, first, last = present(f)
                drain(f, nc + last - first)
            strip_front(f, s, skip)
            return 0

        lax.fori_loop(0, FRONTS, one_front, 0)
        strip_copy(s, acc, out, 1).start()
    for s, _ in tasks:
        strip_copy(s, acc, out, 1).wait()


def extend_add(parent, target, chunks, table, span, tasks):
    count, split = len(chunks), len(chunks[0])
    rows, cols = parent.shape
    nrb, ncb, strips = table_layout(rows, cols)[:3]
    depth = sum(chunk[0].shape[1] for chunk in chunks)
    args = [table, parent, *[a for chunk in chunks for a in chunk]]
    apart = target is not None and target is not parent
    alias = {} if target is None else {1: 0}
    if apart:
        alias = {len(args): 0}
        args.append(target)
    return pl.pallas_call(
        functools.partial(extend_body, count, split, span, tasks, apart),
        grid_spec=pltpu.PrefetchScalarGridSpec(
            num_scalar_prefetch=1,
            grid=(1,),
            in_specs=[HBM] * (len(args) - 1),
            out_specs=HBM,
            scratch_shapes=[
                pltpu.VMEM((rows + BLK, cols), F32),
                pltpu.VMEM((FRONTS, (nrb + TALL) * BLK, depth), HALF),
                pltpu.VMEM((FRONTS, (ncb + WIDE) // WIDE * WIDE * BLK, depth), HALF),
                pltpu.SemaphoreType.DMA((FRONTS,)),
                pltpu.SemaphoreType.DMA((2, strips)),
            ],
        ),
        out_shape=jax.ShapeDtypeStruct((rows, cols), F32),
        input_output_aliases=alias,
        compiler_params=pltpu.CompilerParams(vmem_limit_bytes=60 << 20),
        cost_estimate=pl.CostEstimate(
            flops=rows * cols * depth * len(tasks) // strips,
            bytes_accessed=len(tasks) * (16 << 20),
            transcendentals=0,
        ),
        name="extend_add",
    )(*args)


def paired(size_grp, size_col, flip):
    route = []
    for g in range(size_grp):
        for c in range(size_col):
            to = flip(g, c)
            if to is not None:
                route.append((g * size_col + c, to[0] * size_col + to[1]))
    return route


def fronts_apart(diag_blocks, coupling, parent_front, index_maps):
    ng, nc = lax.axis_size("grp"), lax.axis_size("col")
    nz = nc // 2
    grp, col = lax.axis_index("grp"), lax.axis_index("col")
    width = diag_blocks.shape[1]
    blocks = coupling.shape[1] // width
    per = coupling.shape[0] // BLK
    nrows = parent_front.shape[0] * ng

    def send(block, flip):
        return lax.ppermute(block, ("grp", "col"), paired(ng, nc, flip))

    def along_z(rows, first, last):
        own = lax.slice_in_dim(rows, first * width, last * width, axis=0)
        pile = [own]
        for dz in range(1, nz):
            pile.append(send(own, lambda g, c: (g, c ^ 2 * dz) if c >= first else None))
        return pile

    def across_y(pile):
        near = jnp.concatenate(pile, axis=0)
        return near, send(near, lambda g, c: (g, c ^ 1))

    def one_way(g, c):
        return (g ^ 2, c) if g % 2 == 0 else (g, c ^ 1)

    def other_way(g, c):
        return (g, c ^ 1) if g % 2 == 0 else (g ^ 2, c)

    def other_core(g, c):
        return (g ^ 1, c)

    def advance(stage, held):
        if stage == 0:
            (half,) = held
            line = [send(half, lambda g, c: (g, c ^ 2 * dz)) for dz in range(1, nz)]
            return [jnp.concatenate([half, *line], axis=0)]
        if stage == 1:
            return held + [send(held[0], one_way)]
        if stage == 2:
            return held + [send(a, other_way) for a in held]
        return held + [send(a, other_core) for a in held]

    cuts = [0, 1, 2, *range(4, blocks, 2), blocks]
    spans = list(zip(cuts, cuts[1:]))
    lead = 2
    z_slot = {0: -2, 1: -1, 2: 0}
    y_slot = {0: -1, 1: 0, 2: 1}
    for n in range(3, len(spans)):
        z_slot[n] = 0 if n == len(spans) - 1 else n - 2
        y_slot[n] = z_slot[n] + 1
    band_of = {k: n for n, (a, b) in enumerate(spans) for k in range(a, b)}
    place = jnp.stack([grp, col]).astype(jnp.int32)
    col_id = place[1:]
    span = nz * per
    table = None
    rows_left = diag_blocks
    u_all = x_all = None
    merged = None
    piles, bands = {}, {}
    flying, done, stages = {}, {}, 4
    added = []
    strips = table_layout(*parent_front.shape)[2]
    for slot in range(-lead, blocks + stages):
        for n in flying:
            if done[n] < stages:
                flying[n] = advance(done[n], flying[n])
                done[n] += 1
        for n in range(len(spans)):
            if y_slot[n] == slot:
                bands[n] = across_y(piles.pop(n))
            if z_slot[n] == slot:
                piles[n] = along_z(rows_left, *spans[n])
        if 0 <= slot < blocks:
            n = band_of[slot]
            u_all, x_all, half = factor_step(
                slot, *spans[n], bands[n], coupling, u_all, x_all, col_id
            )
            flying[slot], done[slot] = [half], 0
        if slot == stages:
            table = block_table(index_maps, place, per, span, nrows // BLK, parent_front.shape)
        strip = slot - blocks
        if 0 <= strip < strips and strip < stages - 1:
            ready = [flying[n] for n in range(slot - stages)]
            merged = extend_add(parent_front, merged, ready, table, span, ((strip, 0),))
            added.append(slot - stages)
        flying, piles, bands, u_all, x_all, merged, index_maps, table, rows_left = (
            lax.optimization_barrier(
                (flying, piles, bands, u_all, x_all, merged, index_maps, table, rows_left)
            )
        )
    chunks = [flying[n] for n in range(added[0], blocks)]
    tasks = tuple((n, at - added[0]) for n, at in enumerate(added))
    merged = extend_add(merged, merged, chunks, table, span, tasks)
    mine = lax.dynamic_slice_in_dim(u_all, col * width, width, 0)
    return (merged, mine.T, x_all)


def on_device(diag_blocks, coupling, parent_front, index_maps):
    ng, nc = lax.axis_size("grp"), lax.axis_size("col")
    simple = (
        ng == FRONTS
        and nc % 2 == 0
        and nc & (nc - 1) == 0
        and diag_blocks.shape[1] == BLK
        and coupling.shape[0] % BLK == 0
    )
    body = fronts_apart if simple else general
    return body(diag_blocks, coupling, parent_front, index_maps)


def solution(mesh):
    in_specs = (P("grp", "col"), P(("grp", "col"), None), P("grp", "col"), P())
    out_specs = (P("grp", "col"), P("grp", "col"), P(("grp", "col"), None))
    return jax.shard_map(
        on_device, mesh=mesh, in_specs=in_specs, out_specs=out_specs, check_vma=False
    )
```

```python
import functools

import jax
import jax.numpy as jnp
from jax import lax
from jax.experimental import pallas as pl
from jax.experimental.pallas import tpu as pltpu
from jax.sharding import PartitionSpec as P

FRONTS = 4
BLK = 128
SBLK = 48
PBLK = 96
F32 = jnp.float32
HALF = jnp.bfloat16
EXACT = lax.Precision.HIGHEST
HBM = pl.BlockSpec(memory_space=pltpu.HBM)


def swapped(block, axis, stride):
    count = lax.axis_size(axis)
    route = []
    for low in range(count):
        high = low | 1 << stride
        if high != low and high < count:
            route += [(low, high), (high, low)]
    return lax.ppermute(block, axis, route)


def place_rows(slab_blocks, source_block, present_count, count):
    picked = slab_blocks[jnp.arange(FRONTS)[:, None], source_block]
    picked = jnp.where(present_count[:, :, None, None] > 0, picked, jnp.zeros_like(picked))
    return jnp.transpose(picked, (1, 2, 0, 3)).reshape(count * BLK, -1)


def general(diag_blocks, coupling, parent_front, index_maps):
    groups = lax.axis_size("grp") // FRONTS
    swap_depth = groups.bit_length() - 1
    grp_index = lax.axis_index("grp")
    col_index = lax.axis_index("col")
    gathered = lax.all_gather(diag_blocks, "col", axis=1, tiled=True)
    for bit_pos in range(swap_depth):
        partner = swapped(gathered, "grp", bit_pos)
        is_upper = grp_index // 2**bit_pos % 2 == 1
        lower_half = jnp.where(is_upper, partner, gathered)
        upper_half = jnp.where(is_upper, gathered, partner)
        gathered = jnp.concatenate([lower_half, upper_half], axis=0)
    factor = jnp.linalg.cholesky(gathered)
    rows_here = diag_blocks.shape[0]
    col_width = diag_blocks.shape[1]
    local_start = grp_index % groups * rows_here
    factor_tile = lax.dynamic_slice(
        factor, (local_start, col_index * col_width), (rows_here, col_width)
    )
    panel_rows = lax.linalg.triangular_solve(
        factor, coupling, left_side=False, lower=True, transpose_a=True
    )
    panel_half = panel_rows.astype(HALF)
    panel_tiles = lax.all_to_all(panel_half, "col", split_axis=1, concat_axis=0, tiled=True)
    panel_slab = lax.all_gather(panel_tiles, "grp", axis=0, tiled=True)
    slab_blocks = panel_slab.reshape(FRONTS, SBLK, BLK, -1)
    parent_ids = jnp.arange(PBLK, dtype=jnp.int32)
    matches = (index_maps[:, :, None] == parent_ids[None, None, :]).astype(jnp.int32)
    present_count = jnp.sum(matches, axis=1)
    source_block = jnp.sum(matches * jnp.arange(SBLK, dtype=jnp.int32)[None, :, None], axis=1)
    row_count = parent_front.shape[0]
    contract = (((1,), (1,)), ((), ()))
    every_part = place_rows(slab_blocks, source_block, present_count, PBLK)
    col_operand = lax.all_to_all(every_part, "col", split_axis=0, concat_axis=1, tiled=True)
    row_part = lax.dynamic_slice_in_dim(every_part, grp_index * row_count, row_count, 0)
    update = lax.dot_general(
        lax.all_gather(row_part, "col", axis=1, tiled=True),
        col_operand,
        contract,
        preferred_element_type=F32,
    )
    return (parent_front - update, factor_tile, panel_rows)


def dot(a, b, ca, cb):
    return lax.dot_general(
        a, b, (((ca,), (cb,)), ((), ())), precision=EXACT, preferred_element_type=F32
    )


def eliminate(s_val, u_ref, inv_ref, width):
    rows = 8
    shape = (width, width)
    eye = lax.broadcasted_iota(jnp.int32, shape, 0) == lax.broadcasted_iota(jnp.int32, shape, 1)
    sub = lax.broadcasted_iota(jnp.int32, (rows, width), 0)

    def group(g, carry):
        s, e = carry
        top_s, top_e = s[:rows], e[:rows]
        cols = [jnp.broadcast_to(top_s[:, i : i + 1], (rows, width)) for i in range(rows)]
        u_s = jnp.zeros_like(top_s)
        u_e = jnp.zeros_like(top_e)
        for i in range(rows):
            me = sub == i
            root = lax.rsqrt(cols[i][i : i + 1, :])
            inv = root * root
            u_s = jnp.where(me, top_s * root, u_s)
            u_e = jnp.where(me, top_e * root, u_e)
            for j in range(i + 1, rows):
                w = cols[j][i : i + 1, :] * inv
                cols[j] = jnp.where(me, w, cols[j] - cols[i] * w)
            w_s = top_s[i : i + 1, :] * inv
            w_e = top_e[i : i + 1, :] * inv
            top_s = jnp.where(me, w_s, top_s - cols[i] * w_s)
            top_e = jnp.where(me, w_e, top_e - cols[i] * w_e)
        rest_s, rest_e = s[rows:], e[rows:]
        heads = [rest_s[:, i : i + 1] for i in range(rows)]
        for i in range(rows):
            rest_s = rest_s - heads[i] * top_s[i : i + 1, :]
            rest_e = rest_e - heads[i] * top_e[i : i + 1, :]
        at = pl.multiple_of(g * rows, rows)
        u_ref[pl.ds(at, rows), :] = pltpu.roll(u_s, at, 1)
        inv_ref[pl.ds(at, rows), :] = u_e
        s = jnp.concatenate([rest_s, s[:rows]], axis=0)
        e = jnp.concatenate([rest_e, e[:rows]], axis=0)
        return pltpu.roll(s, width - rows, 1), e

    lax.fori_loop(0, width // rows, group, (s_val, eye.astype(F32)))


def factor_body(k, width, cols, col_ref, *refs):
    pieces, c_ref, refs = refs[:cols], refs[cols], refs[cols + 1 :]
    if k:
        u_in, x_in, refs = refs[0], refs[1], refs[2:]
    u_out, x_out, half_ref, u_v, x_v, s_v, t_v, uk_v, inv_v, sem = refs
    n = s_v.shape[1]
    base = k * width
    rest = n - base - width
    here = pl.ds(base, width)
    if k:
        before = pl.ds(0, base)
        load_u = pltpu.make_async_copy(u_in.at[before, :], u_v.at[before, :], sem.at[0])
        load_x = pltpu.make_async_copy(x_in.at[:, before], x_v.at[:, before], sem.at[1])
        load_u.start()
        load_x.start()
    for rel in range(cols):
        at = pl.multiple_of((col_ref[0] ^ rel) * width, width)
        s_v[:, pl.ds(at, width)] = pieces[rel][...]
    if k:
        load_u.wait()

        def prev(j, _):
            at = pl.multiple_of(j * width, width)
            uj = u_v[pl.ds(at, width), pl.ds(base, n - base)]
            s_v[:, pl.ds(base, n - base)] -= dot(uj[:, :width], uj, 0, 0)
            return 0

        lax.fori_loop(0, k, prev, 0)
    eliminate(s_v[:, here], uk_v, inv_v, width)
    inv = inv_v[...]
    r = lax.broadcasted_iota(jnp.int32, (width, width), 0)
    c = lax.broadcasted_iota(jnp.int32, (width, width), 1)
    if base:
        u_v[here, pl.ds(0, base)] = jnp.zeros((width, base), F32)
    u_v[here, here] = jnp.where(c >= r, uk_v[...], 0.0)
    if rest:
        right = pl.ds(base + width, rest)
        u_v[here, right] = dot(inv, s_v[:, right], 1, 0)
    save_u = pltpu.make_async_copy(u_v.at[here, :], u_out.at[here, :], sem.at[2])
    save_u.start()
    t_v[...] = c_ref[...]
    if k:
        load_x.wait()

        def prevx(j, _):
            at = pl.multiple_of(j * width, width)
            t_v[...] -= dot(x_v[:, pl.ds(at, width)], u_v[pl.ds(at, width), here], 1, 0)
            return 0

        lax.fori_loop(0, k, prevx, 0)
    x_v[:, here] = dot(t_v[...], inv, 1, 1)
    half_ref[...] = x_v[:, here].astype(HALF)
    save_x = pltpu.make_async_copy(x_v.at[:, here], x_out.at[:, here], sem.at[3])
    save_x.start()
    save_u.wait()
    save_x.wait()


def factor_step(k, first, last, band, coupling, u_all, x_all, col_id):
    m, n = coupling.shape
    width = band[0].shape[1]
    cols = n // width
    args, specs = [], []
    for rel in range(cols):
        at = rel // 2 * (last - first) + k - first
        args.append(band[rel % 2])
        specs.append(pl.BlockSpec((width, width), lambda i, s, at=at: (at, 0)))
    args.append(coupling)
    specs += [pl.BlockSpec((m, width), lambda i, s: (0, k))]
    alias = {}
    if k:
        alias = {len(args) + 1: 0, len(args) + 2: 1}
        args += [u_all, x_all]
        specs += [HBM, HBM]
    square = pltpu.VMEM((width, width), F32)
    return pl.pallas_call(
        functools.partial(factor_body, k, width, cols),
        grid_spec=pltpu.PrefetchScalarGridSpec(
            num_scalar_prefetch=1,
            grid=(1,),
            in_specs=specs,
            out_specs=(HBM, HBM, pl.BlockSpec((m, width), lambda i, s: (0, 0))),
            scratch_shapes=[
                pltpu.VMEM((n, n), F32),
                pltpu.VMEM((m, n), F32),
                pltpu.VMEM((width, n), F32),
                pltpu.VMEM((m, width), F32),
                square,
                square,
                pltpu.SemaphoreType.DMA((4,)),
            ],
        ),
        out_shape=(
            jax.ShapeDtypeStruct((n, n), F32),
            jax.ShapeDtypeStruct((m, n), F32),
            jax.ShapeDtypeStruct((m, width), HALF),
        ),
        input_output_aliases=alias,
        compiler_params=pltpu.CompilerParams(vmem_limit_bytes=60 << 20),
        cost_estimate=pl.CostEstimate(
            flops=10**9, bytes_accessed=48 << 20, transcendentals=0
        ),
        name=f"factor{k}",
    )(col_id, *args)


def table_layout(rows, cols):
    nrb, ncb = rows // BLK, cols // BLK
    strips = next(n for n in (3, 2, 1) if nrb % n == 0)
    head = strips + 2
    return nrb, ncb, strips, head, head + 2 * (nrb + ncb)


def table_body(per, span, layout, source, place, table):
    nrb, ncb, strips, head, stride = layout
    grp, col = place[0], place[1]
    x_at, core_at = grp // 2, grp % 2

    def front(f, _):
        base = f * stride

        def entry(where, p, i):
            dc = (f % 2) ^ core_at
            dx = (f // 2) ^ x_at
            dcol = (i // per) ^ col
            dy, dz = dcol % 2, dcol // 2
            near = jnp.where(f % 2 == 0, dx + 2 * dy, dy + 2 * dx)
            table[where] = p
            table[where + 1] = (4 * dc + near) * span + (dz * per + i % per)

        def row(p, n):
            i = source[f, grp * nrb + p]

            @pl.when(p % (nrb // strips) == 0)
            def _():
                table[base + 1 + p // (nrb // strips)] = n

            @pl.when(i >= 0)
            def _():
                entry(base + head + 2 * n, p, i)

            return n + (i >= 0).astype(jnp.int32)

        def column(p, n):
            i = source[f, col * ncb + p]

            @pl.when(i >= 0)
            def _():
                entry(base + head + 2 * (nrb + n), p, i)

            return n + (i >= 0).astype(jnp.int32)

        table[base + 1 + strips] = lax.fori_loop(0, nrb, row, jnp.int32(0))
        table[base] = lax.fori_loop(0, ncb, column, jnp.int32(0))
        return 0

    lax.fori_loop(0, FRONTS, front, 0)


def block_table(index_maps, place, per, span, size, shape):
    layout = table_layout(*shape)
    smem = pl.BlockSpec(memory_space=pltpu.SMEM)
    parents = jnp.arange(size, dtype=jnp.int32)[None, None, :]
    order = jnp.arange(1, index_maps.shape[1] + 1, dtype=jnp.int32)[None, :, None]
    source = jnp.sum(jnp.where(index_maps[:, :, None] == parents, order, 0), axis=1) - 1
    return pl.pallas_call(
        functools.partial(table_body, per, span, layout),
        in_specs=[smem, smem],
        out_specs=smem,
        out_shape=jax.ShapeDtypeStruct((FRONTS * layout[-1],), jnp.int32),
        name="block_table",
    )(source, place)


TALL = 2
WIDE = 4


def extend_body(count, split, span, tasks, aliased, table, parent, *refs):
    arrays, refs = refs[: count * split], refs[count * split :]
    out, acc, lhs, rhs, sem, acc_sem = refs[1:] if aliased else refs
    rows, cols = parent.shape
    nrb, ncb, strips, head, stride = table_layout(rows, cols)
    widths = [arrays[n * split].shape[1] for n in range(count)]

    def strip_copy(s, src, dst, way):
        here = pl.ds(s * (rows // strips), rows // strips)
        return pltpu.make_async_copy(src.at[here, :], dst.at[here, :], acc_sem.at[way, s])

    for s, _ in tasks:
        strip_copy(s, parent, acc, 0).start()

    def bring(f, base, first, last, dst):
        def one(i, _):
            code = table[f * stride + head + 1 + 2 * (base + i)]
            start = pl.multiple_of(code % span * BLK, BLK)
            at = pl.ds(pl.multiple_of(i * BLK, BLK), BLK)
            for a in range(split):

                @pl.when(code // span == a)
                def _():
                    for n in range(count):
                        where = pl.ds(sum(widths[:n]), widths[n])
                        pltpu.make_async_copy(
                            arrays[n * split + a].at[pl.ds(start, BLK), :],
                            dst.at[f, at, where],
                            sem.at[f],
                        ).start()

            return 0

        lax.fori_loop(first, last, one, 0)

    def drain(f, total):
        def one(_, carry):
            block = lhs.at[f, pl.ds(0, BLK), :]
            pltpu.make_async_copy(block, block, sem.at[f]).wait()
            return carry

        lax.fori_loop(0, total, one, 0)

    def present(f):
        first = table[f * stride + 1 + tasks[0][0]]
        last = table[f * stride + 2 + tasks[-1][0]]
        return table[f * stride], first, last

    for f in range(FRONTS):
        nc, first, last = present(f)
        bring(f, 0, first, last, lhs)
        bring(f, nrb, 0, nc, rhs)

    def strip_front(f, s, skip):
        nc = table[f * stride]
        first = table[f * stride + 1 + s]
        last = table[f * stride + 2 + s]
        deep = pl.ds(sum(widths[:skip]), sum(widths[skip:]))

        def col_step(j, _):
            at = pl.multiple_of(j * WIDE * BLK, WIDE * BLK)
            right = rhs[f, pl.ds(at, WIDE * BLK), deep]

            def row_step(i, _):
                top = first + i * TALL
                left = lhs[f, pl.ds(pl.multiple_of(top * BLK, BLK), TALL * BLK), deep]
                prod = lax.dot_general(
                    left, right, (((1,), (1,)), ((), ())), preferred_element_type=F32
                )
                for b in range(WIDE):
                    c = table[f * stride + head + 2 * (nrb + jnp.minimum(j * WIDE + b, ncb - 1))]
                    c = jnp.where(j * WIDE + b < nc, c, 0)
                    for a in range(TALL):
                        r = table[f * stride + head + 2 * jnp.minimum(top + a, nrb - 1)]
                        real = (top + a < last) & (j * WIDE + b < nc)
                        r = jnp.where(real, r, nrb)
                        block = (
                            pl.ds(pl.multiple_of(r * BLK, BLK), BLK),
                            pl.ds(pl.multiple_of(c * BLK, BLK), BLK),
                        )
                        acc[block] -= prod[a * BLK : (a + 1) * BLK, b * BLK : (b + 1) * BLK]

                return 0

            lax.fori_loop(0, (last - first + TALL - 1) // TALL, row_step, 0)
            return 0

        lax.fori_loop(0, (nc + WIDE - 1) // WIDE, col_step, 0)

    for s, skip in tasks:
        strip_copy(s, parent, acc, 0).wait()

        def one_front(f, _):
            if s == tasks[0][0]:
                nc, first, last = present(f)
                drain(f, nc + last - first)
            strip_front(f, s, skip)
            return 0

        lax.fori_loop(0, FRONTS, one_front, 0)
        strip_copy(s, acc, out, 1).start()
    for s, _ in tasks:
        strip_copy(s, acc, out, 1).wait()


def extend_add(parent, target, chunks, table, span, tasks):
    count, split = len(chunks), len(chunks[0])
    rows, cols = parent.shape
    nrb, ncb, strips = table_layout(rows, cols)[:3]
    depth = sum(chunk[0].shape[1] for chunk in chunks)
    args = [table, parent, *[a for chunk in chunks for a in chunk]]
    apart = target is not None and target is not parent
    alias = {} if target is None else {1: 0}
    if apart:
        alias = {len(args): 0}
        args.append(target)
    return pl.pallas_call(
        functools.partial(extend_body, count, split, span, tasks, apart),
        grid_spec=pltpu.PrefetchScalarGridSpec(
            num_scalar_prefetch=1,
            grid=(1,),
            in_specs=[HBM] * (len(args) - 1),
            out_specs=HBM,
            scratch_shapes=[
                pltpu.VMEM((rows + BLK, cols), F32),
                pltpu.VMEM((FRONTS, (nrb + TALL) * BLK, depth), HALF),
                pltpu.VMEM((FRONTS, (ncb + WIDE) // WIDE * WIDE * BLK, depth), HALF),
                pltpu.SemaphoreType.DMA((FRONTS,)),
                pltpu.SemaphoreType.DMA((2, strips)),
            ],
        ),
        out_shape=jax.ShapeDtypeStruct((rows, cols), F32),
        input_output_aliases=alias,
        compiler_params=pltpu.CompilerParams(vmem_limit_bytes=60 << 20),
        cost_estimate=pl.CostEstimate(
            flops=rows * cols * depth * len(tasks) // strips,
            bytes_accessed=len(tasks) * (16 << 20),
            transcendentals=0,
        ),
        name="extend_add",
    )(*args)


def paired(size_grp, size_col, flip):
    route = []
    for g in range(size_grp):
        for c in range(size_col):
            to = flip(g, c)
            if to is not None:
                route.append((g * size_col + c, to[0] * size_col + to[1]))
    return route


def fronts_apart(diag_blocks, coupling, parent_front, index_maps):
    ng, nc = lax.axis_size("grp"), lax.axis_size("col")
    nz = nc // 2
    grp, col = lax.axis_index("grp"), lax.axis_index("col")
    width = diag_blocks.shape[1]
    blocks = coupling.shape[1] // width
    per = coupling.shape[0] // BLK
    nrows = parent_front.shape[0] * ng

    def send(block, flip):
        return lax.ppermute(block, ("grp", "col"), paired(ng, nc, flip))

    def along_z(rows, first, last):
        own = lax.slice_in_dim(rows, first * width, last * width, axis=0)
        pile = [own]
        for dz in range(1, nz):
            pile.append(send(own, lambda g, c: (g, c ^ 2 * dz) if c >= first else None))
        return pile

    def across_y(pile):
        near = jnp.concatenate(pile, axis=0)
        return near, send(near, lambda g, c: (g, c ^ 1))

    def one_way(g, c):
        return (g ^ 2, c) if g % 2 == 0 else (g, c ^ 1)

    def other_way(g, c):
        return (g, c ^ 1) if g % 2 == 0 else (g ^ 2, c)

    def other_core(g, c):
        return (g ^ 1, c)

    def advance(stage, held):
        if stage == 0:
            (half,) = held
            line = [send(half, lambda g, c: (g, c ^ 2 * dz)) for dz in range(1, nz)]
            return [jnp.concatenate([half, *line], axis=0)]
        if stage == 1:
            return held + [send(held[0], one_way)]
        if stage == 2:
            return held + [send(a, other_way) for a in held]
        return held + [send(a, other_core) for a in held]

    cuts = [0, 1, 2, *range(4, blocks, 2), blocks]
    spans = list(zip(cuts, cuts[1:]))
    lead = 2
    z_slot = {0: -2, 1: -1, 2: 0}
    y_slot = {0: -1, 1: 0, 2: 1}
    for n in range(3, len(spans)):
        z_slot[n] = 0 if n == len(spans) - 1 else n - 2
        y_slot[n] = z_slot[n] + 1
    band_of = {k: n for n, (a, b) in enumerate(spans) for k in range(a, b)}
    place = jnp.stack([grp, col]).astype(jnp.int32)
    col_id = place[1:]
    span = nz * per
    table = None
    rows_left = diag_blocks
    u_all = x_all = None
    merged = None
    piles, bands = {}, {}
    flying, done, stages = {}, {}, 4
    added = []
    strips = table_layout(*parent_front.shape)[2]
    for slot in range(-lead, blocks + stages):
        for stage in (2, 1, 0, 3):
            for n in [n for n in flying if done[n] == stage]:
                flying[n] = advance(stage, flying[n])
                done[n] = -stage - 1
        done = {n: abs(stage) for n, stage in done.items()}
        for n in range(len(spans)):
            if y_slot[n] == slot:
                bands[n] = across_y(piles.pop(n))
            if z_slot[n] == slot:
                piles[n] = along_z(rows_left, *spans[n])
        if 0 <= slot < blocks:
            n = band_of[slot]
            u_all, x_all, half = factor_step(
                slot, *spans[n], bands[n], coupling, u_all, x_all, col_id
            )
            flying[slot], done[slot] = [half], 0
        if slot == -1:
            table = block_table(index_maps, place, per, span, nrows // BLK, parent_front.shape)
        strip = slot - blocks
        if 0 <= strip < strips and strip < stages - 1:
            ready = [flying[n] for n in range(slot - stages)]
            merged = extend_add(parent_front, merged, ready, table, span, ((strip, 0),))
            added.append(slot - stages)
        turn = sorted(flying, key=lambda n: (3, 2, 1, 0, 4).index(done[n]))
        held = [flying[n] for n in turn]
        held, piles, bands, u_all, x_all, merged, index_maps, table, rows_left = (
            lax.optimization_barrier(
                (held, piles, bands, u_all, x_all, merged, index_maps, table, rows_left)
            )
        )
        flying = dict(sorted(zip(turn, held)))
    chunks = [flying[n] for n in range(added[0], blocks)]
    tasks = tuple((n, at - added[0]) for n, at in enumerate(added))
    merged = extend_add(merged, merged, chunks, table, span, tasks)
    mine = lax.dynamic_slice_in_dim(u_all, col * width, width, 0)
    return (merged, mine.T, x_all)


def on_device(diag_blocks, coupling, parent_front, index_maps):
    ng, nc = lax.axis_size("grp"), lax.axis_size("col")
    simple = (
        ng == FRONTS
        and nc % 2 == 0
        and nc & (nc - 1) == 0
        and diag_blocks.shape[1] == BLK
        and coupling.shape[0] % BLK == 0
    )
    body = fronts_apart if simple else general
    return body(diag_blocks, coupling, parent_front, index_maps)


def solution(mesh):
    in_specs = (P("grp", "col"), P(("grp", "col"), None), P("grp", "col"), P())
    out_specs = (P("grp", "col"), P("grp", "col"), P(("grp", "col"), None))
    return jax.shard_map(
        on_device, mesh=mesh, in_specs=in_specs, out_specs=out_specs, check_vma=False
    )
```
